32 devices in a mesh: src: 4 (over y, x), tile: 8 (over z, core).
Axes of the slice: x: 2, y: 2, z: 4, core: 2. Of those that a mesh axis runs over, the one named last changes fastest.
Arguments:
- latent: bfloat16 [3, 32, 16, 160], P(None, ('src', 'tile')), may hold values from -6 to 6
- row_map: int32 [32], replicated, may hold values from 0 to 31, each once
- latent_cache: bfloat16 [2, 32, 16, 160], P(None, 'tile'), may hold values from -6 to 6
- cache_one: bfloat16 [2, 32, 384, 160], P(None, 'tile', 'src'), may hold values from -5 to 5
- cache_two: bfloat16 [2, 32, 384, 160], P(None, 'tile', 'src'), may hold values from -5 to 5
- conv_in_w: bfloat16 [3, 3, 3, 16, 384], P(None, None, None, None, 'src'), may hold values from -0.3125 to 0.3125
- weight_one: bfloat16 [3, 3, 3, 384, 384], P(None, None, None, 'src'), may hold values from -0.0625 to 0.0625
- weight_two: bfloat16 [3, 3, 3, 384, 384], P(None, None, None, 'src'), may hold values from -0.0625 to 0.0625
- gain_one: float32 [384], P('src'), may hold values from 0.1 to 1.9
- gain_two: float32 [384], P('src'), may hold values from 0.1 to 1.9
Outputs:
- decoded: bfloat16 [3, 32, 384, 160], P(None, 'tile', 'src')
The draws below stay inside these ranges and needn't reach their ends.
All inputs are finite; a program needn't handle non-finite values.
Results may differ from the reference program's by a relative error of at most 0.0037.
The reference program's roundings to bfloat16 on the way count: a program that leaves them out, or rounds other values in their place, can miss the bound.
Values may be sent and summed in bfloat16 or wider, within the bound.
No kernel may reach another device: no remote copies, remote signals or barrier semaphores. Data moves between devices by JAX's collectives and lax.ppermute only.
A program may use at most 128 MiB of HBM per device.

```python
import jax
import jax.numpy as jnp
from jax import lax

LC = 16
C = 384
GROUPS = 32
LW = 160
FR = 3
GSIZE = 12
LH = 32


def steps_of(stream_key, shape, split, smallest, top_value):
    def one(position, blocks):
        heights = jax.random.uniform(jax.random.fold_in(jax.random.fold_in(stream_key, 6), position), (blocks,), jnp.float32, smallest / len(split), top_value / len(split))
        return jnp.repeat(jnp.exp(heights), shape[position] // blocks).reshape((-1,) + (1,) * (len(shape) - position - 1))

    level = one(*split[0])
    for cut in split[1:]:
        level = level * one(*cut)
    return level


def normal_values(own_key, shape, scale, reach, shards=(), kind=jnp.bfloat16):
    entries = jax.random.normal(own_key, shape, jnp.float32) * scale
    if len(shards) > 0:
        entries = steps_of(own_key, shape, shards, -0.22, 0.18) * entries
    return jnp.clip(entries, min=-reach, max=reach).astype(kind)


def setup_inputs(seed: int = 0) -> dict:
    key_of = jax.random.split(jax.random.key(seed), 11)
    return {
        "latent": normal_values(key_of[0], (FR, LH, LC, LW), 1.0, 6.0, ((1, 32),)),
        "row_map": jax.random.permutation(key_of[1], LH).astype(jnp.int32),
        "latent_cache": normal_values(key_of[2], (2, LH, LC, LW), 1.0, 6.0, ((1, 8),)),
        "cache_one": normal_values(key_of[3], (2, LH, C, LW), 0.7, 5.0, ((1, 8), (2, 4))),
        "cache_two": normal_values(key_of[4], (2, LH, C, LW), 0.7, 5.0, ((1, 8), (2, 4))),
        "conv_in_w": normal_values(key_of[5], (3, 3, 3, LC, C), (27 * LC) ** -0.5, 0.3125, ((4, 4),)),
        "weight_one": normal_values(key_of[6], (3, 3, 3, C, C), (27 * C) ** -0.5, 0.0625, ((3, 4),)),
        "weight_two": normal_values(key_of[7], (3, 3, 3, C, C), (27 * C) ** -0.5, 0.0625, ((3, 4),)),
        "gain_one": jnp.clip(1.0 + 0.18 * jax.random.normal(key_of[8], (C,), jnp.float32), 0.1, 1.9),
        "gain_two": jnp.clip(1.0 + 0.18 * jax.random.normal(key_of[9], (C,), jnp.float32), 0.1, 1.9),
    }


def causal_conv(frames, weight):
    frame_count = frames.shape[0] - 2
    row_count = frames.shape[1]
    columns = frames.shape[3]
    padded = jnp.pad(frames, ((0, 0), (1, 1), (0, 0), (1, 1)))
    summed = jnp.zeros((frame_count, row_count, weight.shape[4], columns), jnp.float32)
    for tap_time in range(3):
        for tap_row in range(3):
            for tap_col in range(3):
                window = padded[tap_time:tap_time + frame_count, tap_row:tap_row + row_count, :, tap_col:tap_col + columns].astype(jnp.float32)
                summed = summed + jnp.einsum('fhcw,co->fhow', window, weight[tap_time, tap_row, tap_col].astype(jnp.float32))
    return summed

def group_norm(hidden, gain):
    frame_count, row_count, channels, columns = hidden.shape
    shaped = hidden.reshape(frame_count, row_count, GROUPS, GSIZE, columns)
    group_mean = lax.optimization_barrier(jnp.mean(shaped, axis=(0, 1, 3, 4), keepdims=True))
    centred = shaped - group_mean
    spread = lax.optimization_barrier(jnp.mean(centred * centred, axis=(0, 1, 3, 4), keepdims=True))
    normed = (centred * lax.rsqrt(spread + 1e-06)).reshape(hidden.shape)
    normed = normed * gain.astype(jnp.float32)[None, None, :, None]
    return jax.nn.silu(normed).astype(jnp.bfloat16)

def reference(latent, row_map, latent_cache, cache_one, cache_two, conv_in_w, weight_one, weight_two, gain_one, gain_two):
    grid = jnp.zeros_like(latent).at[:, row_map].set(latent)
    first = causal_conv(jnp.concatenate([latent_cache, grid], axis=0), conv_in_w).astype(jnp.bfloat16)
    act_one = group_norm(first.astype(jnp.float32), gain_one)
    middle = causal_conv(jnp.concatenate([cache_one, act_one], axis=0), jnp.transpose(weight_one, (0, 1, 2, 4, 3)))
    act_two = group_norm(middle, gain_two)
    last = causal_conv(jnp.concatenate([cache_two, act_two], axis=0), jnp.transpose(weight_two, (0, 1, 2, 4, 3)))
    return (first.astype(jnp.float32) + last).astype(jnp.bfloat16)
```

```python
import functools

import jax
import jax.numpy as jnp
from jax import lax
from jax.experimental import pallas as pl
from jax.experimental.pallas import tpu as pltpu
from jax.sharding import PartitionSpec as P

GSIZE = 12
F32 = jnp.float32
BF16 = jnp.bfloat16
VMEM = pl.BlockSpec(memory_space=pltpu.VMEM)
SMEM = pl.BlockSpec(memory_space=pltpu.SMEM)


def call(body, outs, name, flops=0, scratch=(), specs=None, n_in=0):
    return pl.pallas_call(
        body,
        out_shape=outs,
        in_specs=specs if specs is not None else [VMEM] * n_in,
        out_specs=jax.tree.map(lambda _: VMEM, outs),
        scratch_shapes=list(scratch),
        name=name,
        cost_estimate=pl.CostEstimate(flops=flops, bytes_accessed=1 << 20, transcendentals=0),
        compiler_params=pltpu.CompilerParams(vmem_limit_bytes=40 << 20),
    )


def xor_send(x, axis, mask):
    return lax.ppermute(x, axis, [(i, i ^ mask) for i in range(lax.axis_size(axis))])


def xor_stage(x, axis, masks):
    return [x] + [xor_send(x, axis, m) for m in masks]


def far_masks(size):
    low, stages = 2, []
    while low < size:
        if low * 2 < size:
            stages.append([low, 2 * low, 3 * low])
            low *= 4
        else:
            stages.append([low])
            low *= 2
    return stages


def to_next(x):
    return lax.ppermute(x, "tile", [(i, i + 1) for i in range(lax.axis_size("tile") - 1)])


def to_previous(x):
    return lax.ppermute(x, "tile", [(i + 1, i) for i in range(lax.axis_size("tile") - 1)])


def pack_body(one_ref, two_ref, out_ref):
    frames, rows, channels, _ = one_ref.shape
    for n, ref in enumerate((one_ref, two_ref)):
        for f in range(frames):
            parts = [ref[f, h].astype(F32).T for h in range(rows)]
            out_ref[n * frames + f] = jnp.concatenate(parts, axis=1).astype(BF16)


def weights_body(src_ref, w_ref, late_ref, early_ref, turned):
    outs, ins = w_ref.shape[3], w_ref.shape[4]
    mine = src_ref[0]
    late_ref[...] = jnp.zeros_like(late_ref)
    early_ref[...] = jnp.zeros_like(early_ref)

    def tap(n, _):
        b, e = n // 3, n % 3
        for a in range(3):
            turned[...] = w_ref[a, b, e].astype(F32).T
            for slot in range(ins // outs):
                start = pl.multiple_of(jnp.bitwise_xor(mine, slot) * outs, 8)
                rows = turned[pl.ds(start, outs), :].astype(BF16)
                here = pl.ds(slot * outs, outs)
                if a == 2:
                    late_ref[n, here, 0:outs] = rows
                if a == 1:
                    late_ref[n, here, 128 : 128 + outs] = rows
                    early_ref[n, here, 0:outs] = rows
                if a == 0:
                    early_ref[n, here, 128 : 128 + outs] = rows
        return 0

    lax.fori_loop(0, 9, tap, 0)


def first_body(tab_ref, near_ref, far_ref, cache_ref, w0, w1, w2, w3, first_ref, stat_ref, taps, wall):
    half = near_ref.shape[0]
    rows = cache_ref.shape[0]
    columns = cache_ref.shape[2] // 2
    frames = near_ref.shape[2] // columns
    wall[...] = jnp.concatenate([w[...].astype(F32) for w in (w0, w1, w2, w3)], axis=1).astype(BF16)
    lane = lax.broadcasted_iota(jnp.int32, (16, columns), 1)
    for row in range(rows):
        place = tab_ref[row]
        kept = tab_ref[rows + row].astype(F32)
        inner = jnp.where(place >= half, place - half, place)
        new = jnp.where(place >= half, far_ref[inner].astype(F32), near_ref[inner].astype(F32)) * kept
        old = cache_ref[row].astype(F32)
        for f in range(frames + 2):
            v = old[:, f * columns : (f + 1) * columns] if f < 2 else new[:, (f - 2) * columns : (f - 1) * columns]
            zero = jnp.zeros((16, 1), F32)
            left = jnp.concatenate([zero, v[:, : columns - 1]], axis=1)
            right = jnp.concatenate([v[:, 1:], zero], axis=1)
            taps[row, f] = jnp.concatenate([left, v, right], axis=0).astype(BF16)
    total = jnp.zeros((8, wall.shape[1]), F32)
    for t in range(frames):
        for r in range(rows - 2):
            patch = jnp.concatenate([taps[r + b, t + a] for a in range(3) for b in range(3)], axis=0)
            got = lax.dot_general(patch, wall[...], (((0,), (0,)), ((), ())), preferred_element_type=F32).astype(BF16)
            first_ref[t, r] = got
            if 0 < r < rows - 3:
                total += jnp.sum(got.astype(F32).reshape(columns // 8, 8, -1), axis=0)
    count = frames * (rows - 4) * columns
    mean = jnp.sum(total, axis=0, keepdims=True) * (1.0 / count)
    square = jnp.zeros((8, wall.shape[1]), F32)
    for t in range(frames):
        for r in range(1, rows - 3):
            d = first_ref[t, r].astype(F32) - mean
            square += jnp.sum((d * d).reshape(columns // 8, 8, -1), axis=0)
    stat_ref[0:1, :] = mean
    stat_ref[1:2, :] = jnp.sum(square, axis=0, keepdims=True)


def scale_shift(means, squares, gain, count):
    channels = gain.shape[1]
    lane = lax.broadcasted_iota(jnp.int32, (channels, channels), 0) // GSIZE
    other = lax.broadcasted_iota(jnp.int32, (channels, channels), 1) // GSIZE
    same = (lane == other).astype(F32)

    def over_group(v):
        v = jnp.broadcast_to(v, (8, channels))
        return jnp.dot(v, same, precision=lax.Precision.HIGHEST, preferred_element_type=F32)[0:1]

    tiles = sum(m.shape[0] for m in means)
    mean = over_group(sum(jnp.sum(m, axis=0, keepdims=True) for m in means)) * (1.0 / (tiles * GSIZE))
    spread = jnp.zeros_like(mean)
    for m, q in zip(means, squares):
        spread += jnp.sum(q + float(count) * (m - mean) * (m - mean), axis=0, keepdims=True)
    variance = over_group(spread) * (1.0 / (count * tiles * GSIZE))
    scale = lax.rsqrt(variance + 1e-06) * gain
    return mean, scale


def put_row(taps, f, r, v):
    columns, channels = v.shape
    at = lax.broadcasted_iota(jnp.int32, v.shape, 0)
    left = jnp.where(at == 0, 0.0, pltpu.roll(v, 1, axis=0))
    right = jnp.where(at == columns - 1, 0.0, pltpu.roll(v, columns - 1, axis=0))
    taps[f, r, :, 0:channels] = left.astype(BF16)
    taps[f, r, :, channels : 2 * channels] = v.astype(BF16)
    taps[f, r, :, 2 * channels :] = right.astype(BF16)


def activate(v, mean, scale):
    y = (v - mean) * scale
    return (0.5 * y) * (1.0 + jnp.tanh(0.5 * y))


def tap_product(taps, f, w_ref, lanes):
    frames, rows, columns, depth = taps.shape
    summed = None
    for b in range(3):
        x = taps[f, b : b + rows - 2].reshape((rows - 2) * columns, depth)
        w = w_ref[3 * b : 3 * b + 3, :, lanes].reshape(depth, lanes.stop - lanes.start)
        got = jnp.dot(x, w, preferred_element_type=F32)
        summed = got if summed is None else summed + got
    return summed


def spread_rows(own, up, down, f, r, rows, channels):
    if r == 0:
        return up[f].astype(F32)
    if r == rows - 1:
        return down[f].astype(F32)
    lanes = slice((r - 1) * channels, r * channels)
    return jnp.concatenate([piece[f, :, lanes].astype(F32) for piece in own], axis=1)


def cached_body(base, p0, p1, p2, p3, up, down, early_ref, out_ref, taps):
    rows = taps.shape[1]
    channels = p0.shape[2] // (rows - 2)
    for f in range(2):
        for r in range(rows):
            put_row(taps, f, r, spread_rows((p0, p1, p2, p3), up, down, base + f, r, rows, channels))
    out_ref[0] = tap_product(taps, 0, early_ref, slice(128, 256))
    both = tap_product(taps, 1, early_ref, slice(0, 256))
    out_ref[0] += both[:, 0:128]
    out_ref[1] = both[:, 128:256]


def conv_current(taps, late_ref, early_ref, cached_ref):
    both = tap_product(taps, 0, late_ref, slice(0, 256))
    yield cached_ref[0] + both[:, 0:128]
    middle = cached_ref[1] + both[:, 128:256]
    last = tap_product(taps, 0, early_ref, slice(128, 256))
    both = tap_product(taps, 1, late_ref, slice(0, 256))
    yield middle + both[:, 0:128]
    last = last + both[:, 128:256]
    yield last + tap_product(taps, 2, late_ref, slice(0, 128))


def middle_body(n_stats, count, edge_ref, *refs):
    stats, (gain_ref, first_ref, cached_ref, late_ref, early_ref, out_ref, stat_ref, taps, kept) = refs[:n_stats], refs[n_stats:]
    means = [s[:, 0, :] for s in stats]
    squares = [s[:, 1, :] for s in stats]
    mean, scale = scale_shift(means, squares, gain_ref[...], count)
    frames, rows, columns, _ = taps.shape
    for f in range(frames):
        for r in range(rows):
            v = activate(first_ref[f, r].astype(F32), mean, scale)
            if r == 0:
                v = v * edge_ref[0].astype(F32)
            if r == rows - 1:
                v = v * edge_ref[1].astype(F32)
            put_row(taps, f, r, v)
    channels = out_ref.shape[2] // (rows - 2)
    total = jnp.zeros((1, 128), F32)
    for f, got in enumerate(conv_current(taps, late_ref, early_ref, cached_ref)):
        kept[f] = got
        total += jnp.sum(got, axis=0, keepdims=True)
        parts = [got[h * columns : (h + 1) * columns, 0:channels] for h in range(rows - 2)]
        out_ref[f] = jnp.concatenate(parts, axis=1).astype(BF16)
    local = total * (1.0 / (frames * (rows - 2) * columns))
    square = jnp.zeros((1, 128), F32)
    for f in range(frames):
        d = kept[f] - local
        square += jnp.sum(d * d, axis=0, keepdims=True)
    stat_ref[0:1, :] = local
    stat_ref[1:2, :] = square


def last_body(n_stats, count, edge_ref, *refs):
    stats = refs[:n_stats]
    (gain_ref, p0, p1, p2, p3, up, down, first_ref, cached_ref, late_ref, early_ref, out_ref, taps) = refs[n_stats:]
    frames, rows, columns, _ = taps.shape
    channels = p0.shape[2] // (rows - 2)

    def wide(s, n):
        return jnp.concatenate([s[:, slot, n, 0:channels] for slot in range(4)], axis=1)

    means = [wide(s, 0) for s in stats]
    squares = [wide(s, 1) for s in stats]
    mean, scale = scale_shift(means, squares, gain_ref[...], count)
    for f in range(frames):
        for r in range(rows):
            v = activate(spread_rows((p0, p1, p2, p3), up, down, f, r, rows, channels), mean, scale)
            if r == 0:
                v = v * edge_ref[0].astype(F32)
            if r == rows - 1:
                v = v * edge_ref[1].astype(F32)
            put_row(taps, f, r, v)
    for f, got in enumerate(conv_current(taps, late_ref, early_ref, cached_ref)):
        for h in range(rows - 2):
            here = got[h * columns : (h + 1) * columns, 0:channels]
            here = here + first_ref[f, h + 1][:, 0:channels].astype(F32)
            out_ref[f, h] = here.T.astype(BF16)


def edges_of(pieces, channels):
    top = jnp.concatenate([p[:, :, :channels] for p in pieces], axis=2)
    bottom = jnp.concatenate([p[:, :, -channels:] for p in pieces], axis=2)
    return to_next(bottom), to_previous(top)


def per_device(
    latent,
    row_map,
    latent_cache,
    cache_one,
    cache_two,
    conv_in_w,
    weight_one,
    weight_two,
    gain_one,
    gain_two,
):
    frames, _, lc, columns = latent.shape
    tile_rows = latent_cache.shape[1]
    tiles, sources = lax.axis_size("tile"), lax.axis_size("src")
    channels = conv_in_w.shape[4]
    wide = channels * sources
    s, t = lax.axis_index("src"), lax.axis_index("tile")
    src = jnp.stack([s, t]).astype(jnp.int32)

    targets = t * tile_rows - 2 + jnp.arange(tile_rows + 4, dtype=jnp.int32)
    found = row_map[None, :] == targets[:, None]
    index = jnp.sum(jnp.where(found, jnp.arange(row_map.shape[0], dtype=jnp.int32)[None, :], 0), axis=1)
    to_t = jnp.bitwise_xor(index % tiles, t)
    to_s = jnp.bitwise_xor(index // tiles, s)
    half = tiles // 2 * sources
    place = (to_t & 1) * half + (to_t >> 1) * sources + to_s
    table = jnp.concatenate([place, jnp.any(found, axis=1).astype(jnp.int32)]).astype(jnp.int32)
    edge = jnp.stack([t > 0, t < tiles - 1]).astype(jnp.int32)

    row = latent[:, 0].transpose(1, 0, 2).reshape(lc, frames * columns).astype(F32)
    gains = jnp.concatenate([gain_one, gain_two])
    gains = jnp.pad(gains, (0, frames * columns - 2 * channels))
    message = jnp.concatenate([row, jnp.broadcast_to(gains[None], (8, frames * columns))], axis=0)
    got = jnp.stack(xor_stage(message, "src", range(1, sources)))
    near = got[:, :lc].astype(BF16)
    gain_a = got[:, lc, :channels].reshape(1, wide)
    gain_b = got[:, lc, channels : 2 * channels].reshape(1, wide)
    for masks in far_masks(tiles):
        near = jnp.concatenate(xor_stage(near, "tile", masks), axis=0)
    far = xor_send(near, "tile", 1)

    w_in = xor_stage(conv_in_w.reshape(27 * lc, channels), "src", range(1, sources))
    span = latent_cache.transpose(1, 2, 0, 3).reshape(tile_rows, lc, 2 * columns)
    span = jnp.concatenate([to_next(span[-2:]), span, to_previous(span[:2])], axis=0)

    packed = call(pack_body, jax.ShapeDtypeStruct((4, columns, tile_rows * channels), BF16), "pack", n_in=2)(
        cache_one, cache_two
    )
    pieces = xor_stage(packed, "src", range(1, sources))
    up, down = edges_of(pieces, channels)

    def turn(w, name):
        shape = jax.ShapeDtypeStruct((9, wide, 256), BF16)
        return call(
            weights_body, (shape, shape), name, scratch=[pltpu.VMEM((wide, channels), F32)], specs=[SMEM, VMEM]
        )(src, w)

    late_one, early_one = turn(weight_one, "turn_one")
    late_two, early_two = turn(weight_two, "turn_two")

    rows = tile_rows + 2
    spots = tile_rows * columns
    flops = 2 * 27 * wide * channels * spots

    def cached(base, early, name):
        return call(
            functools.partial(cached_body, base),
            jax.ShapeDtypeStruct((2, spots, 128), F32),
            name,
            flops=flops,
            scratch=[pltpu.VMEM((2, rows, columns, 3 * wide), BF16)],
            n_in=7,
        )(*pieces, up, down, early)

    cached_one = cached(0, early_one, "cached_one")
    cached_two = cached(2, early_two, "cached_two")

    first, stat = call(
        first_body,
        (jax.ShapeDtypeStruct((frames, rows, columns, wide), BF16), jax.ShapeDtypeStruct((2, wide), F32)),
        "first",
        flops=flops // 4,
        scratch=[
            pltpu.VMEM((rows + 2, frames + 2, 3 * lc, columns), BF16),
            pltpu.VMEM((27 * lc, wide), BF16),
        ],
        specs=[SMEM] + [VMEM] * 7,
    )(table, near, far, span, *w_in)

    def over_tiles(x):
        x = jnp.stack(xor_stage(x, "tile", [1]))
        stages = far_masks(tiles)
        for masks in stages[:-1]:
            x = jnp.concatenate(xor_stage(x, "tile", masks), axis=0)
        return xor_stage(x, "tile", stages[-1])

    count = frames * spots
    stats = over_tiles(stat)
    middle, stat_two = call(
        functools.partial(middle_body, len(stats), count),
        (jax.ShapeDtypeStruct((frames, columns, tile_rows * channels), BF16), jax.ShapeDtypeStruct((2, 128), F32)),
        "middle",
        flops=flops * 2,
        scratch=[
            pltpu.VMEM((frames, rows, columns, 3 * wide), BF16),
            pltpu.VMEM((frames, spots, 128), F32),
        ],
        specs=[SMEM] + [VMEM] * (len(stats) + 5),
    )(edge, *stats, gain_a, first, cached_one, late_one, early_one)

    mids = xor_stage(middle, "src", range(1, sources))
    stats = over_tiles(jnp.stack(xor_stage(stat_two, "src", range(1, sources))))
    above, below = edges_of(mids, channels)
    return call(
        functools.partial(last_body, len(stats), count),
        jax.ShapeDtypeStruct((frames, tile_rows, channels, columns), BF16),
        "last",
        flops=flops * 2,
        scratch=[pltpu.VMEM((frames, rows, columns, 3 * wide), BF16)],
        specs=[SMEM] + [VMEM] * (len(stats) + 11),
    )(edge, *stats, gain_b, *mids, above, below, first, cached_two, late_two, early_two)


def solution(mesh):
    placed = (
        P(None, ("src", "tile"), None, None),
        P(),
        P(None, "tile", None, None),
        P(None, "tile", "src", None),
        P(None, "tile", "src", None),
        P(None, None, None, None, "src"),
        P(None, None, None, "src", None),
        P(None, None, None, "src", None),
        P("src"),
        P("src"),
    )
    return jax.shard_map(
        per_device,
        mesh=mesh,
        in_specs=placed,
        out_specs=P(None, "tile", "src", None),
        check_vma=False,
    )
```

```python
import functools

import jax
import jax.numpy as jnp
from jax import lax
from jax.experimental import pallas as pl
from jax.experimental.pallas import tpu as pltpu
from jax.sharding import PartitionSpec as P


GSIZE = 12
F32 = jnp.float32
BF16 = jnp.bfloat16
VMEM_LIMIT = 24 << 20
VMEM = pl.BlockSpec(memory_space=pltpu.VMEM)
SMEM = pl.BlockSpec(memory_space=pltpu.SMEM)
HBM = pl.BlockSpec(memory_space=pl.ANY)


def call(body, outs, flops=0, scratch=(), specs=None, n_in=0, out_specs=None, limit=VMEM_LIMIT):
    return pl.pallas_call(
        body,
        out_shape=outs,
        in_specs=specs if specs is not None else [VMEM] * n_in,
        out_specs=out_specs if out_specs is not None else jax.tree.map(lambda _: VMEM, outs),
        scratch_shapes=list(scratch),
        cost_estimate=pl.CostEstimate(flops=flops, bytes_accessed=1 << 20, transcendentals=0),
        compiler_params=pltpu.CompilerParams(vmem_limit_bytes=limit),
    )


def xor_send(x, axis, mask):
    return lax.ppermute(x, axis, [(i, i ^ mask) for i in range(lax.axis_size(axis))])


def xor_stage(x, axis, masks):
    return [x] + [xor_send(x, axis, m) for m in masks]


def far_masks(size):
    low, stages = 2, []
    while low < size:
        if low * 2 < size:
            stages.append([low, 2 * low, 3 * low])
            low *= 4
        else:
            stages.append([low])
            low *= 2
    return stages


def to_next(x):
    return lax.ppermute(x, "tile", [(i, i + 1) for i in range(lax.axis_size("tile") - 1)])


def to_previous(x):
    return lax.ppermute(x, "tile", [(i + 1, i) for i in range(lax.axis_size("tile") - 1)])


def fetch(sources, targets, sems):
    copies = [pltpu.make_async_copy(src, dst, sems.at[n]) for n, (src, dst) in enumerate(zip(sources, targets))]
    for copy in copies:
        copy.start()
    for copy in copies:
        copy.wait()


def message_body(*refs):
    out_ref, latent_ref, gain_a, gain_b, sems = refs[3:]
    fetch(refs[:3], (latent_ref, gain_a, gain_b), sems)
    lc, channels = latent_ref.shape[2], gain_a.shape[1]
    line = jnp.concatenate([latent_ref[f, 0].astype(F32) for f in range(latent_ref.shape[0])], axis=1)
    gains = jnp.concatenate([gain_a[...], gain_b[...]], axis=1)
    out_ref[0:lc, :] = line
    out_ref[lc:, :] = jnp.zeros_like(out_ref[lc:, :])
    out_ref[lc : lc + 1, 0 : 2 * channels] = gains


def pack_body(*refs):
    packed_ref, own_ref, low_ref, high_ref, *here, sems = refs[3:]
    fetch(refs[:3], here, sems)
    one_ref, two_ref, span_ref = here
    frames, rows = one_ref.shape[0], one_ref.shape[1]
    columns, lc = one_ref.shape[2], span_ref.shape[2]

    def joined(parts):
        return jnp.concatenate([part.astype(F32) for part in parts], axis=1).astype(BF16)

    every = [ref.at[f] for ref in (one_ref, two_ref) for f in range(frames)]
    for n, ref in enumerate(every):
        packed_ref[n] = joined([ref[h] for h in range(rows)])
    low_ref[0:columns, :] = joined([ref[0] for ref in every])
    high_ref[0:columns, :] = joined([ref[rows - 1] for ref in every])
    width = span_ref.shape[3] * frames
    for ref in (low_ref, high_ref):
        ref[columns:, :] = jnp.zeros_like(ref[columns:, :])
    for row in range(rows):
        both = joined([span_ref[f, row] for f in range(frames)])
        own_ref[row] = both
        if row < 2:
            low_ref[columns + row * lc : columns + (row + 1) * lc, 0:width] = both
        if row >= rows - 2:
            at = columns + (row - rows + 2) * lc
            high_ref[at : at + lc, 0:width] = both


def rim_body(packed_ref, before, after, one_ref, two_ref):
    columns = packed_ref.shape[1]
    channels = packed_ref.shape[2] // 4
    for n, ref in enumerate((one_ref, two_ref)):
        parts = []
        for f in range(2):
            ref[f] = packed_ref[2 * n + f]
            lanes = slice((2 * n + f) * channels, (2 * n + f + 1) * channels)
            parts += [side[0:columns, lanes].astype(F32) for side in (before, after)]
        ref[2] = jnp.concatenate(parts, axis=1).astype(BF16)


def weights_body(w_ref, late_ref, early_ref, turned):
    outs, ins = w_ref.shape[3], w_ref.shape[4]
    mine = lax.axis_index("src")
    late_ref[...] = jnp.zeros_like(late_ref)
    early_ref[...] = jnp.zeros_like(early_ref)

    def tap(n, _):
        b, e = n // 3, n % 3
        for a in range(3):
            turned[...] = w_ref[a, b, e].astype(F32).T
            for slot in range(ins // outs):
                start = pl.multiple_of(jnp.bitwise_xor(mine, slot) * outs, 8)
                rows = turned[pl.ds(start, outs), :].astype(BF16)
                here = pl.ds(slot * outs, outs)
                if a == 2:
                    late_ref[n, here, 0:outs] = rows
                if a == 1:
                    late_ref[n, here, 128 : 128 + outs] = rows
                    early_ref[n, here, 0:outs] = rows
                if a == 0:
                    early_ref[n, here, 128 : 128 + outs] = rows
        return 0

    lax.fori_loop(0, 9, tap, 0)


def first_body(map_ref, near_ref, far_ref, before, own, after, w0, w1, w2, w3, first_ref, stat_ref, taps, wall, tab_ref):
    half = near_ref.shape[0]
    rows = own.shape[0] + 4
    columns = own.shape[2] // 2
    frames = near_ref.shape[2] // columns
    s, t, tiles = lax.axis_index("src"), lax.axis_index("tile"), lax.axis_size("tile")
    top = t * (rows - 4) - 2
    for row in range(rows):
        tab_ref[row] = -1
    for i in range(map_ref.shape[0]):
        at = map_ref[i] - top
        to_t, to_s = jnp.bitwise_xor(i % tiles, t), jnp.bitwise_xor(i // tiles, s)
        place = to_t % 2 * half + to_t // 2 * 4 + to_s

        @pl.when(jnp.logical_and(at >= 0, at < rows))
        def _():
            tab_ref[jnp.clip(at, 0, rows - 1)] = place

    wall[...] = jnp.concatenate([w[...].astype(F32) for w in (w0, w1, w2, w3)], axis=1).astype(BF16)
    for row in range(rows):
        place = tab_ref[row]
        kept = (place >= 0).astype(F32)
        inner = jnp.maximum(jnp.where(place >= half, place - half, place), 0)
        new = jnp.where(place >= half, far_ref[inner].astype(F32), near_ref[inner].astype(F32)) * kept
        if 2 <= row < rows - 2:
            old = own[row - 2].astype(F32)
        else:
            at = columns + 16 * (row if row < 2 else row - rows + 2)
            old = (before if row < 2 else after)[at : at + 16, 0 : 2 * columns].astype(F32)
        for f in range(frames + 2):
            v = old[:, f * columns : (f + 1) * columns] if f < 2 else new[:, (f - 2) * columns : (f - 1) * columns]
            zero = jnp.zeros((16, 1), F32)
            left = jnp.concatenate([zero, v[:, : columns - 1]], axis=1)
            right = jnp.concatenate([v[:, 1:], zero], axis=1)
            taps[row, f] = jnp.concatenate([left, v, right], axis=0).astype(BF16)
    total = jnp.zeros((8, wall.shape[1]), F32)
    for t in range(frames):
        for r in range(rows - 2):
            patch = jnp.concatenate([taps[r + b, t + a] for a in range(3) for b in range(3)], axis=0)
            got = lax.dot_general(patch, wall[...], (((0,), (0,)), ((), ())), preferred_element_type=F32).astype(BF16)
            first_ref[t, r] = got
            if 0 < r < rows - 3:
                total += jnp.sum(got.astype(F32).reshape(columns // 8, 8, -1), axis=0)
    count = frames * (rows - 4) * columns
    mean = jnp.sum(total, axis=0, keepdims=True) * (1.0 / count)
    square = jnp.zeros((8, wall.shape[1]), F32)
    for t in range(frames):
        for r in range(1, rows - 3):
            d = first_ref[t, r].astype(F32) - mean
            square += jnp.sum((d * d).reshape(columns // 8, 8, -1), axis=0)
    stat_ref[0:1, :] = mean
    stat_ref[1:2, :] = jnp.sum(square, axis=0, keepdims=True)


def scale_shift(means, squares, gain, count):
    channels = gain.shape[1]
    lane = lax.broadcasted_iota(jnp.int32, (channels, channels), 0) // GSIZE
    other = lax.broadcasted_iota(jnp.int32, (channels, channels), 1) // GSIZE
    same = (lane == other).astype(F32)

    def over_group(v):
        v = jnp.broadcast_to(v, (8, channels))
        return jnp.dot(v, same, precision=lax.Precision.HIGHEST, preferred_element_type=F32)[0:1]

    tiles = sum(m.shape[0] for m in means)
    mean = over_group(sum(jnp.sum(m, axis=0, keepdims=True) for m in means)) * (1.0 / (tiles * GSIZE))
    spread = jnp.zeros_like(mean)
    for m, q in zip(means, squares):
        spread += jnp.sum(q + float(count) * (m - mean) * (m - mean), axis=0, keepdims=True)
    variance = over_group(spread) * (1.0 / (count * tiles * GSIZE))
    scale = lax.rsqrt(variance + 1e-06) * gain
    return mean, scale


def put_row(taps, f, r, v):
    columns, channels = v.shape
    at = lax.broadcasted_iota(jnp.int32, v.shape, 0)
    left = jnp.where(at == 0, 0.0, pltpu.roll(v, 1, axis=0))
    right = jnp.where(at == columns - 1, 0.0, pltpu.roll(v, columns - 1, axis=0))
    taps[f, r, :, 0:channels] = left.astype(BF16)
    taps[f, r, :, channels : 2 * channels] = v.astype(BF16)
    taps[f, r, :, 2 * channels :] = right.astype(BF16)


def activate(v, mean, scale):
    y = (v - mean) * scale
    return (0.5 * y) * (1.0 + jnp.tanh(0.5 * y))


def tap_product(taps, f, w_ref, lanes):
    _, rows, columns, depth = taps.shape
    summed = None
    for b in range(3):
        x = taps[f, b : b + rows - 2].reshape((rows - 2) * columns, depth)
        w = w_ref[3 * b : 3 * b + 3, :, lanes].reshape(depth, lanes.stop - lanes.start)
        got = jnp.dot(x, w, preferred_element_type=F32)
        summed = got if summed is None else summed + got
    return summed


def spread_rows(own, up, down, f, r, rows, channels):
    if r == 0:
        return up[f].astype(F32)
    if r == rows - 1:
        return down[f].astype(F32)
    lanes = slice((r - 1) * channels, r * channels)
    return jnp.concatenate([piece[f, :, lanes].astype(F32) for piece in own], axis=1)


def cached_body(p0, p1, p2, p3, early_ref, out_ref, taps):
    pieces = (p0, p1, p2, p3)
    rows = taps.shape[1]
    channels = p0.shape[2] // (rows - 2)
    for f in range(2):
        for r in range(rows):
            if 0 < r < rows - 1:
                v = spread_rows(pieces, None, None, f, r, rows, channels)
            else:
                at = (2 * f + (r > 0)) * channels
                v = jnp.concatenate([piece[2, :, at : at + channels].astype(F32) for piece in pieces], axis=1)
            put_row(taps, f, r, v)
    one = tap_product(taps, 0, early_ref, slice(128, 256))
    both = tap_product(taps, 1, early_ref, slice(0, 256))
    out_ref[0] = one + both[:, 0:128]
    out_ref[1] = both[:, 128:256]


def conv_current(taps, late_ref, early_ref, cached_ref):
    both = tap_product(taps, 0, late_ref, slice(0, 256))
    yield cached_ref[0] + both[:, 0:128]
    middle = cached_ref[1] + both[:, 128:256]
    last = tap_product(taps, 0, early_ref, slice(128, 256))
    both = tap_product(taps, 1, late_ref, slice(0, 256))
    yield middle + both[:, 0:128]
    last = last + both[:, 128:256]
    yield last + tap_product(taps, 2, late_ref, slice(0, 128))


def gain_of(refs, n, channels):
    at = refs[0].shape[0] - 8
    lanes = slice(n * channels, (n + 1) * channels)
    return jnp.concatenate([ref[at : at + 1, lanes] for ref in refs], axis=1)


def inside():
    t = lax.axis_index("tile")
    return (t > 0).astype(F32), (t < lax.axis_size("tile") - 1).astype(F32)


def middle_body(n_stats, count, *refs):
    stats = refs[:n_stats]
    gains = refs[n_stats : n_stats + 4]
    first_ref, cached_ref, late_ref, early_ref, out_ref, stat_ref, taps, kept = refs[n_stats + 4 :]
    edges = inside()
    means = [s[:, 0, :] for s in stats]
    squares = [s[:, 1, :] for s in stats]
    mean, scale = scale_shift(means, squares, gain_of(gains, 0, first_ref.shape[3] // 4), count)
    frames, rows, columns, _ = taps.shape
    for f in range(frames):
        for r in range(rows):
            v = activate(first_ref[f, r].astype(F32), mean, scale)
            if r == 0:
                v = v * edges[0]
            if r == rows - 1:
                v = v * edges[1]
            put_row(taps, f, r, v)
    channels = out_ref.shape[2] // (rows - 2)
    total = jnp.zeros((1, 128), F32)
    for f, got in enumerate(conv_current(taps, late_ref, early_ref, cached_ref)):
        kept[f] = got
        total += jnp.sum(got, axis=0, keepdims=True)
        parts = [got[h * columns : (h + 1) * columns, 0:channels] for h in range(rows - 2)]
        out_ref[f] = jnp.concatenate(parts, axis=1).astype(BF16)
    local = total * (1.0 / (frames * (rows - 2) * columns))
    square = jnp.zeros((1, 128), F32)
    for f in range(frames):
        d = kept[f] - local
        square += jnp.sum(d * d, axis=0, keepdims=True)
    stat_ref[0:1, :] = local
    stat_ref[1:2, :] = square


def last_body(n_stats, count, *refs):
    stats = refs[:n_stats]
    gains, (p0, p1, p2, p3) = refs[n_stats : n_stats + 4], refs[n_stats + 4 : n_stats + 8]
    cached_ref, late_ref, early_ref, out_ref, scale_ref, taps = refs[n_stats + 8 :]
    frames, rows, _, _ = taps.shape
    channels = p0.shape[2] // (rows - 2)

    def wide(s, n):
        return jnp.concatenate([s[:, slot, n, 0:channels] for slot in range(4)], axis=1)

    means = [wide(s, 0) for s in stats]
    squares = [wide(s, 1) for s in stats]
    mean, scale = scale_shift(means, squares, gain_of(gains, 1, channels), count)
    scale_ref[0:1, :] = mean
    scale_ref[1:2, :] = scale
    for f in range(frames):
        taps[f, 0] = jnp.zeros_like(taps[f, 0])
        taps[f, rows - 1] = jnp.zeros_like(taps[f, rows - 1])
        for r in range(1, rows - 1):
            v = spread_rows((p0, p1, p2, p3), None, None, f, r, rows, channels)
            put_row(taps, f, r, activate(v, mean, scale))
    for f, got in enumerate(conv_current(taps, late_ref, early_ref, cached_ref)):
        out_ref[f] = got


def edge_body(part_ref, scale_ref, up, down, first_ref, late_ref, early_ref, out_hbm, taps, out_ref, sems):
    frames, _, columns, depth = taps.shape
    rows = first_ref.shape[1]
    channels = out_ref.shape[3]
    mean, scale = scale_ref[0:1, :], scale_ref[1:2, :]
    added = []
    for side, (ref, kept, b) in enumerate(zip((up, down), inside(), (0, 2))):
        for f in range(frames):
            put_row(taps, f, side, activate(ref[f].astype(F32), mean, scale) * kept)
        taken = slice(3 * b, 3 * b + 3)
        x = jnp.concatenate([taps[f, side] for f in range(frames)], axis=0)
        both = jnp.dot(x, late_ref[taken].reshape(depth, 256), preferred_element_type=F32)
        late = jnp.dot(taps[0, side], early_ref[taken, :, 128:256].reshape(depth, 128), preferred_element_type=F32)
        now, then = both[:, 0:128], both[:, 128:256]
        added.append(
            [
                now[0:columns],
                now[columns : 2 * columns] + then[0:columns],
                now[2 * columns :] + then[columns : 2 * columns] + late,
            ]
        )
    for f in range(frames):
        for h in range(rows - 2):
            here = part_ref[f, h * columns : (h + 1) * columns]
            if h == 0:
                here = here + added[0][f]
            if h == rows - 3:
                here = here + added[1][f]
            here = here[:, 0:channels] + first_ref[f, h + 1][:, 0:channels].astype(F32)
            out_ref[f, h] = here.astype(BF16)
        pltpu.make_async_copy(out_ref.at[f], out_hbm.at[f], sems.at[f]).start()
    for f in range(frames):
        pltpu.make_async_copy(out_ref.at[f], out_hbm.at[f], sems.at[f]).wait()


def edges_of(pieces, channels):
    top = jnp.concatenate([p[:, :, :channels] for p in pieces], axis=2)
    bottom = jnp.concatenate([p[:, :, -channels:] for p in pieces], axis=2)
    return to_next(bottom), to_previous(top)


def shaped(shape, dtype):
    return jax.ShapeDtypeStruct(tuple(shape), dtype)


def window(
    latent,
    row_map,
    latent_cache,
    cache_one,
    cache_two,
    conv_in_w,
    weight_one,
    weight_two,
    gain_one,
    gain_two,
):
    frames, _, lc, columns = latent.shape
    tile_rows = latent_cache.shape[1]
    tiles, sources = lax.axis_size("tile"), lax.axis_size("src")
    channels = conv_in_w.shape[4]
    wide = channels * sources
    others = range(1, sources)

    message = call(
        message_body,
        shaped((lc + 8, frames * columns), F32),
        scratch=[
            pltpu.VMEM(latent.shape, BF16),
            pltpu.VMEM((1, channels), F32),
            pltpu.VMEM((1, channels), F32),
            pltpu.SemaphoreType.DMA((3,)),
        ],
        specs=[HBM] * 3,
        limit=60 * 1024 * 1024,
    )(latent, gain_one[None], gain_two[None])
    got = xor_stage(message, "src", others)
    near = jnp.stack([x[:lc].astype(BF16) for x in got])
    for masks in far_masks(tiles):
        near = jnp.concatenate(xor_stage(near, "tile", masks), axis=0)
    far = xor_send(near, "tile", 1)

    w_in = xor_stage(conv_in_w.reshape(27 * lc, channels), "src", others)
    caches = (cache_one.transpose(0, 1, 3, 2), cache_two.transpose(0, 1, 3, 2), latent_cache)
    strip = shaped((columns + 2 * lc, tile_rows * channels), BF16)
    packed, span, low, high = call(
        pack_body,
        (shaped((4, columns, tile_rows * channels), BF16), shaped((tile_rows, lc, 2 * columns), BF16), strip, strip),
        scratch=[pltpu.VMEM(x.shape, BF16) for x in caches] + [pltpu.SemaphoreType.DMA((3,))],
        specs=[HBM] * 3,
        limit=60 * 1024 * 1024,
    )(*caches)
    before = to_next(high)
    after = to_previous(low)
    rimmed = shaped((3, columns, tile_rows * channels), BF16)
    rim_one, rim_two = call(rim_body, (rimmed, rimmed), n_in=3)(packed, before, after)
    pieces_one = xor_stage(rim_one, "src", others)
    pieces_two = xor_stage(rim_two, "src", others)

    def turn(w):
        shape = shaped((9, wide, 256), BF16)
        return call(weights_body, (shape, shape), scratch=[pltpu.VMEM((wide, channels), F32)], n_in=1)(w)

    late_one, early_one = turn(weight_one)
    late_two, early_two = turn(weight_two)

    rows = tile_rows + 2
    spots = tile_rows * columns
    flops = 2 * 27 * wide * channels * spots

    def cached(pieces, early):
        return call(
            cached_body,
            shaped((2, spots, 128), F32),
            flops=flops,
            scratch=[pltpu.VMEM((2, rows, columns, 3 * wide), BF16)],
            n_in=5,
        )(*pieces, early)

    cached_one = cached(pieces_one, early_one)
    cached_two = cached(pieces_two, early_two)

    first, stat = call(
        first_body,
        (shaped((frames, rows, columns, wide), BF16), shaped((2, wide), F32)),
        flops=flops // 4,
        scratch=[
            pltpu.VMEM((rows + 2, frames + 2, 3 * lc, columns), BF16),
            pltpu.VMEM((27 * lc, wide), BF16),
            pltpu.SMEM((rows + 2,), jnp.int32),
        ],
        specs=[SMEM] + [VMEM] * 9,
    )(row_map, near, far, before, span, after, *w_in)

    def over_tiles(x):
        x = jnp.stack(xor_stage(x, "tile", [1]))
        stages = far_masks(tiles)
        for masks in stages[:-1]:
            x = jnp.concatenate(xor_stage(x, "tile", masks), axis=0)
        return xor_stage(x, "tile", stages[-1])

    count = frames * spots
    stats = over_tiles(stat)
    middle, stat_two = call(
        functools.partial(middle_body, len(stats), count),
        (shaped((frames, columns, tile_rows * channels), BF16), shaped((2, 128), F32)),
        flops=flops * 2,
        scratch=[
            pltpu.VMEM((frames, rows, columns, 3 * wide), BF16),
            pltpu.VMEM((frames, spots, 128), F32),
        ],
        n_in=len(stats) + 8,
    )(*stats, *got, first, cached_one, late_one, early_one)

    mids = xor_stage(middle, "src", others)
    stats = over_tiles(jnp.stack(xor_stage(stat_two, "src", others)))
    above, below = edges_of(mids, channels)
    part, scales = call(
        functools.partial(last_body, len(stats), count),
        (shaped((frames, spots, 128), F32), shaped((2, wide), F32)),
        flops=flops * 2,
        scratch=[pltpu.VMEM((frames, rows, columns, 3 * wide), BF16)],
        n_in=len(stats) + 11,
    )(*stats, *got, *mids, cached_two, late_two, early_two)
    decoded = call(
        edge_body,
        shaped((frames, tile_rows, columns, channels), BF16),
        flops=flops // 2,
        scratch=[
            pltpu.VMEM((frames, 2, columns, 3 * wide), BF16),
            pltpu.VMEM((frames, tile_rows, columns, channels), BF16),
            pltpu.SemaphoreType.DMA((frames,)),
        ],
        n_in=7,
        out_specs=HBM,
    )(part, scales, above, below, first, late_two, early_two)
    return decoded.transpose(0, 1, 3, 2)


def solution(mesh):
    placed = (
        P(None, ("src", "tile"), None, None),
        P(),
        P(None, "tile", None, None),
        P(None, "tile", "src", None),
        P(None, "tile", "src", None),
        P(None, None, None, None, "src"),
        P(None, None, None, "src", None),
        P(None, None, None, "src", None),
        P("src"),
        P("src"),
    )
    return jax.shard_map(
        window,
        mesh=mesh,
        in_specs=placed,
        out_specs=P(None, "tile", "src", None),
        check_vma=False,
    )
```

```python
import functools

import jax
import jax.numpy as jnp
from jax import lax
from jax.experimental import pallas as pl
from jax.experimental.pallas import tpu as pltpu
from jax.sharding import PartitionSpec as P


GSIZE = 12
F32 = jnp.float32
BF16 = jnp.bfloat16
VMEM_LIMIT = 24 << 20
VMEM = pl.BlockSpec(memory_space=pltpu.VMEM)
SMEM = pl.BlockSpec(memory_space=pltpu.SMEM)
HBM = pl.BlockSpec(memory_space=pl.ANY)


def call(body, outs, flops=0, scratch=(), specs=None, n_in=0, out_specs=None, limit=VMEM_LIMIT, alias=None):
    return pl.pallas_call(
        body,
        out_shape=outs,
        in_specs=specs if specs is not None else [VMEM] * n_in,
        out_specs=out_specs if out_specs is not None else jax.tree.map(lambda _: VMEM, outs),
        scratch_shapes=list(scratch),
        input_output_aliases=alias or {},
        cost_estimate=pl.CostEstimate(flops=flops, bytes_accessed=1 << 20, transcendentals=0),
        compiler_params=pltpu.CompilerParams(vmem_limit_bytes=limit),
    )


def xor_send(x, axis, mask):
    return lax.ppermute(x, axis, [(i, i ^ mask) for i in range(lax.axis_size(axis))])


def xor_stage(x, axis, masks):
    return [x] + [xor_send(x, axis, m) for m in masks]


def far_masks(size):
    low, stages = 2, []
    while low < size:
        if low * 2 < size:
            stages.append([low, 2 * low, 3 * low])
            low *= 4
        else:
            stages.append([low])
            low *= 2
    return stages


def stay(*arrays):
    return [pltpu.with_memory_space_constraint(x, pltpu.HBM) for x in arrays]


def to_next(x):
    return lax.ppermute(x, "tile", [(i, i + 1) for i in range(lax.axis_size("tile") - 1)])


def to_previous(x):
    return lax.ppermute(x, "tile", [(i + 1, i) for i in range(lax.axis_size("tile") - 1)])


def fetch(sources, targets, sems):
    copies = [pltpu.make_async_copy(src, dst, sems.at[n]) for n, (src, dst) in enumerate(zip(sources, targets))]
    for copy in copies:
        copy.start()
    for copy in copies:
        copy.wait()


GROUP = 5


def message_body(*refs):
    out_ref, latent_ref, gain_a, gain_b, w_ref, sems = refs[4:]
    fetch(refs[:4], (latent_ref, gain_a, gain_b, w_ref), sems)
    lc, channels = latent_ref.shape[2], gain_a.shape[1]

    def joined(parts):
        return jnp.concatenate([part.astype(F32) for part in parts], axis=1).astype(BF16)

    out_ref[0:lc, :] = joined([latent_ref[f, 0] for f in range(latent_ref.shape[0])])
    taps = w_ref.shape[0] // lc
    for n in range(0, taps, GROUP):
        held = [w_ref[k * lc : (k + 1) * lc] for k in range(n, min(n + GROUP, taps))]
        at = lc + n // GROUP * lc
        out_ref[at : at + lc, 0 : len(held) * channels] = joined(held)
    gains = jnp.concatenate([gain_a[...], gain_b[...]], axis=1)
    at = out_ref.shape[0] - 16
    terms = []
    for _ in range(3):
        terms.append(gains.astype(BF16).astype(F32))
        gains = gains - terms[-1]
    rows = jnp.concatenate(terms + [jnp.zeros((13, gains.shape[1]), F32)], axis=0)
    out_ref[at:, 0 : gains.shape[1]] = rows.astype(BF16)


def near_body(*refs):
    out_ref = refs[-1]
    for n, ref in enumerate(refs[:-1]):
        out_ref[n] = ref[0 : out_ref.shape[1], :]


def pack_body(*refs):
    own_one, own_two, span_out, low_ref, high_ref, *here, sems = refs[3:]
    fetch(refs[:3], here, sems)
    one_ref, two_ref, span_ref = here
    frames, rows = one_ref.shape[0], one_ref.shape[1]
    columns, lc = one_ref.shape[2], span_ref.shape[2]

    def joined(parts):
        return jnp.concatenate([part.astype(F32) for part in parts], axis=1).astype(BF16)

    for ref, out in ((one_ref, own_one), (two_ref, own_two)):
        for f in range(frames):
            out[f] = joined([ref[f, h] for h in range(rows)])
    every = [ref.at[f] for ref in (one_ref, two_ref) for f in range(frames)]
    low_ref[0:columns, :] = joined([ref[0] for ref in every])
    high_ref[0:columns, :] = joined([ref[rows - 1] for ref in every])
    width = span_ref.shape[3] * frames
    for ref in (low_ref, high_ref):
        ref[columns:, :] = jnp.zeros_like(ref[columns:, :])
    for row in range(rows):
        both = joined([span_ref[f, row] for f in range(frames)])
        span_out[row] = both
        if row < 2:
            low_ref[columns + row * lc : columns + (row + 1) * lc, 0:width] = both
        if row >= rows - 2:
            at = columns + (row - rows + 2) * lc
            high_ref[at : at + lc, 0:width] = both


def rim_body(one_in, two_in, before, after, one_out, two_out, held, sems):
    columns = held.shape[1]
    channels = held.shape[2] // 4
    copies = []
    for n, out in enumerate((one_out, two_out)):
        parts = []
        for f in range(2):
            lanes = slice((2 * n + f) * channels, (2 * n + f + 1) * channels)
            parts += [side[0:columns, lanes].astype(F32) for side in (before, after)]
        held[n] = jnp.concatenate(parts, axis=1).astype(BF16)
        copies.append(pltpu.make_async_copy(held.at[n], out.at[2], sems.at[n]))
        copies[-1].start()
    for copy in copies:
        copy.wait()


def weights_body(w_ref, late_ref, early_ref, turned):
    outs, ins = w_ref.shape[3], w_ref.shape[4]
    mine = lax.axis_index("src")
    turned[...] = jnp.zeros_like(turned)

    def tap(n, _):
        b, e = n // 3, n % 3
        for a in range(3):
            turned[a, :, 0:outs] = w_ref[a, b, e].astype(F32).T
        for slot in range(ins // outs):
            start = pl.multiple_of(jnp.bitwise_xor(mine, slot) * outs, 8)
            here = pl.ds(slot * outs, outs)
            early, middle, late = [turned[a, pl.ds(start, outs), :].astype(BF16) for a in range(3)]
            late_ref[n, here, 0:128] = late
            late_ref[n, here, 128:256] = middle
            early_ref[n, here, 0:128] = middle
            early_ref[n, here, 128:256] = early
        return 0

    lax.fori_loop(0, 9, tap, 0)


def first_body(map_ref, near_ref, far_ref, before, own, after, m0, m1, m2, m3, first_ref, stat_ref, taps, wall, tab_ref):
    half = near_ref.shape[0]
    rows = own.shape[0] + 4
    columns = own.shape[2] // 2
    frames = near_ref.shape[2] // columns
    s, t, tiles = lax.axis_index("src"), lax.axis_index("tile"), lax.axis_size("tile")
    top = t * (rows - 4) - 2
    for row in range(rows):
        tab_ref[row] = -1
    for i in range(map_ref.shape[0]):
        at = map_ref[i] - top
        to_t, to_s = jnp.bitwise_xor(i % tiles, t), jnp.bitwise_xor(i // tiles, s)
        place = to_t % 2 * half + to_t // 2 * 4 + to_s

        @pl.when(jnp.logical_and(at >= 0, at < rows))
        def _():
            tab_ref[jnp.clip(at, 0, rows - 1)] = place

    wide = wall.shape[1]
    for n in range(wall.shape[0] // 16):
        at, lanes = 16 + n // GROUP * 16, slice(n % GROUP * wide // 4, (n % GROUP + 1) * wide // 4)
        parts = [m[at : at + 16, lanes].astype(F32) for m in (m0, m1, m2, m3)]
        wall[16 * n : 16 * n + 16, :] = jnp.concatenate(parts, axis=1).astype(BF16)
    for row in range(rows):
        place = tab_ref[row]
        kept = (place >= 0).astype(F32)
        inner = jnp.maximum(jnp.where(place >= half, place - half, place), 0)
        new = jnp.where(place >= half, far_ref[inner].astype(F32), near_ref[inner].astype(F32)) * kept
        if 2 <= row < rows - 2:
            old = own[row - 2].astype(F32)
        else:
            at = columns + 16 * (row if row < 2 else row - rows + 2)
            old = (before if row < 2 else after)[at : at + 16, 0 : 2 * columns].astype(F32)
        for f in range(frames + 2):
            v = old[:, f * columns : (f + 1) * columns] if f < 2 else new[:, (f - 2) * columns : (f - 1) * columns]
            zero = jnp.zeros((16, 1), F32)
            left = jnp.concatenate([zero, v[:, : columns - 1]], axis=1)
            right = jnp.concatenate([v[:, 1:], zero], axis=1)
            taps[row, f] = jnp.concatenate([left, v, right], axis=0).astype(BF16)
    total = jnp.zeros((8, wall.shape[1]), F32)
    for t in range(frames):
        for r in range(rows - 2):
            patch = jnp.concatenate([taps[r + b, t + a] for a in range(3) for b in range(3)], axis=0)
            got = lax.dot_general(patch, wall[...], (((0,), (0,)), ((), ())), preferred_element_type=F32).astype(BF16)
            first_ref[t, r] = got
            if 0 < r < rows - 3:
                total += jnp.sum(got.astype(F32).reshape(columns // 8, 8, -1), axis=0)
    count = frames * (rows - 4) * columns
    mean = jnp.sum(total, axis=0, keepdims=True) * (1.0 / count)
    square = jnp.zeros((8, wall.shape[1]), F32)
    for t in range(frames):
        for r in range(1, rows - 3):
            d = first_ref[t, r].astype(F32) - mean
            square += jnp.sum((d * d).reshape(columns // 8, 8, -1), axis=0)
    stat_ref[0:1, :] = mean
    stat_ref[1:2, :] = jnp.sum(square, axis=0, keepdims=True)


def scale_shift(means, squares, gain, count):
    channels = gain.shape[1]
    lane = lax.broadcasted_iota(jnp.int32, (channels, channels), 0) // GSIZE
    other = lax.broadcasted_iota(jnp.int32, (channels, channels), 1) // GSIZE
    same = (lane == other).astype(F32)

    def over_group(v):
        v = jnp.broadcast_to(v, (8, channels))
        return jnp.dot(v, same, precision=lax.Precision.HIGHEST, preferred_element_type=F32)[0:1]

    tiles = sum(m.shape[0] for m in means)
    mean = over_group(sum(jnp.sum(m, axis=0, keepdims=True) for m in means)) * (1.0 / (tiles * GSIZE))
    spread = jnp.zeros_like(mean)
    for m, q in zip(means, squares):
        spread += jnp.sum(q + float(count) * (m - mean) * (m - mean), axis=0, keepdims=True)
    variance = over_group(spread) * (1.0 / (count * tiles * GSIZE))
    scale = lax.rsqrt(variance + 1e-06) * gain
    return mean, scale


def put_row(taps, f, r, v):
    columns, channels = v.shape
    at = lax.broadcasted_iota(jnp.int32, v.shape, 0)
    left = jnp.where(at == 0, 0.0, pltpu.roll(v, 1, axis=0))
    right = jnp.where(at == columns - 1, 0.0, pltpu.roll(v, columns - 1, axis=0))
    taps[f, r, :, 0:channels] = left.astype(BF16)
    taps[f, r, :, channels : 2 * channels] = v.astype(BF16)
    taps[f, r, :, 2 * channels :] = right.astype(BF16)


def activate(v, mean, scale):
    y = (v - mean) * scale
    return (0.5 * y) * (1.0 + jnp.tanh(0.5 * y))


def tap_product(taps, f, w_ref, lanes):
    _, rows, columns, depth = taps.shape
    summed = None
    for b in range(3):
        x = taps[f, b : b + rows - 2].reshape((rows - 2) * columns, depth)
        w = w_ref[3 * b : 3 * b + 3, :, lanes].reshape(depth, lanes.stop - lanes.start)
        got = jnp.dot(x, w, preferred_element_type=F32)
        summed = got if summed is None else summed + got
    return summed


def spread_rows(own, up, down, f, r, rows, channels):
    if r == 0:
        return up[f].astype(F32)
    if r == rows - 1:
        return down[f].astype(F32)
    lanes = slice((r - 1) * channels, r * channels)
    return jnp.concatenate([piece[f, :, lanes].astype(F32) for piece in own], axis=1)


def cached_body(p0, p1, p2, p3, early_ref, out_ref, taps):
    pieces = (p0, p1, p2, p3)
    rows = taps.shape[1]
    channels = p0.shape[2] // (rows - 2)
    for f in range(2):
        for r in range(rows):
            if 0 < r < rows - 1:
                v = spread_rows(pieces, None, None, f, r, rows, channels)
            else:
                at = (2 * f + (r > 0)) * channels
                v = jnp.concatenate([piece[2, :, at : at + channels].astype(F32) for piece in pieces], axis=1)
            put_row(taps, f, r, v)
    one = tap_product(taps, 0, early_ref, slice(128, 256))
    both = tap_product(taps, 1, early_ref, slice(0, 256))
    out_ref[0] = one + both[:, 0:128]
    out_ref[1] = both[:, 128:256]


def conv_current(taps, late_ref, early_ref, cached_ref):
    both = tap_product(taps, 0, late_ref, slice(0, 256))
    yield cached_ref[0] + both[:, 0:128]
    middle = cached_ref[1] + both[:, 128:256]
    last = tap_product(taps, 0, early_ref, slice(128, 256))
    both = tap_product(taps, 1, late_ref, slice(0, 256))
    yield middle + both[:, 0:128]
    last = last + both[:, 128:256]
    yield last + tap_product(taps, 2, late_ref, slice(0, 128))


def gain_of(refs, n, channels):
    at = refs[0].shape[0] - 16
    lanes = slice(n * channels, (n + 1) * channels)
    terms = [ref[at : at + 16, lanes].astype(F32) for ref in refs]
    return jnp.concatenate([(t[0:1] + t[1:2]) + t[2:3] for t in terms], axis=1)


def inside():
    t = lax.axis_index("tile")
    return (t > 0).astype(F32), (t < lax.axis_size("tile") - 1).astype(F32)


def middle_body(n_stats, count, *refs):
    stats = refs[:n_stats]
    gains = refs[n_stats : n_stats + 4]
    first_ref, cached_ref, late_ref, early_ref, out_ref, stat_ref, taps, kept = refs[n_stats + 4 :]
    edges = inside()
    means = [s[:, 0, :] for s in stats]
    squares = [s[:, 1, :] for s in stats]
    mean, scale = scale_shift(means, squares, gain_of(gains, 0, first_ref.shape[3] // 4), count)
    frames, rows, columns, _ = taps.shape
    for f in range(frames):
        for r in range(rows):
            v = activate(first_ref[f, r].astype(F32), mean, scale)
            if r == 0:
                v = v * edges[0]
            if r == rows - 1:
                v = v * edges[1]
            put_row(taps, f, r, v)
    channels = out_ref.shape[2] // (rows - 2)
    total = jnp.zeros((1, 128), F32)
    for f, got in enumerate(conv_current(taps, late_ref, early_ref, cached_ref)):
        kept[f] = got
        total += jnp.sum(got, axis=0, keepdims=True)
        parts = [got[h * columns : (h + 1) * columns, 0:channels] for h in range(rows - 2)]
        out_ref[f] = jnp.concatenate(parts, axis=1).astype(BF16)
    local = total * (1.0 / (frames * (rows - 2) * columns))
    square = jnp.zeros((1, 128), F32)
    for f in range(frames):
        d = kept[f] - local
        square += jnp.sum(d * d, axis=0, keepdims=True)
    stat_ref[0:1, :] = local
    stat_ref[1:2, :] = square


def last_body(n_stats, count, *refs):
    stats = refs[:n_stats]
    gains, (p0, p1, p2, p3) = refs[n_stats : n_stats + 4], refs[n_stats + 4 : n_stats + 8]
    cached_ref, late_ref, early_ref, out_ref, scale_ref, taps = refs[n_stats + 8 :]
    frames, rows, _, _ = taps.shape
    channels = p0.shape[2] // (rows - 2)

    def wide(s, n):
        return jnp.concatenate([s[:, slot, n, 0:channels] for slot in range(4)], axis=1)

    means = [wide(s, 0) for s in stats]
    squares = [wide(s, 1) for s in stats]
    mean, scale = scale_shift(means, squares, gain_of(gains, 1, channels), count)
    scale_ref[0:1, :] = mean
    scale_ref[1:2, :] = scale
    for f in range(frames):
        taps[f, 0] = jnp.zeros_like(taps[f, 0])
        taps[f, rows - 1] = jnp.zeros_like(taps[f, rows - 1])
        for r in range(1, rows - 1):
            v = spread_rows((p0, p1, p2, p3), None, None, f, r, rows, channels)
            put_row(taps, f, r, activate(v, mean, scale))
    for f, got in enumerate(conv_current(taps, late_ref, early_ref, cached_ref)):
        out_ref[f] = got


def edge_body(part_ref, scale_ref, up, down, first_ref, late_ref, early_ref, out_hbm, taps, out_ref, sems):
    frames, _, columns, depth = taps.shape
    rows = first_ref.shape[1]
    channels = out_ref.shape[3]
    mean, scale = scale_ref[0:1, :], scale_ref[1:2, :]
    added = []
    for side, (ref, kept, b) in enumerate(zip((up, down), inside(), (0, 2))):
        for f in range(frames):
            put_row(taps, f, side, activate(ref[f].astype(F32), mean, scale) * kept)
        taken = slice(3 * b, 3 * b + 3)
        x = jnp.concatenate([taps[f, side] for f in range(frames)], axis=0)
        both = jnp.dot(x, late_ref[taken].reshape(depth, 256), preferred_element_type=F32)
        late = jnp.dot(taps[0, side], early_ref[taken, :, 128:256].reshape(depth, 128), preferred_element_type=F32)
        now, then = both[:, 0:128], both[:, 128:256]
        added.append(
            [
                now[0:columns],
                now[columns : 2 * columns] + then[0:columns],
                now[2 * columns :] + then[columns : 2 * columns] + late,
            ]
        )
    for f in range(frames):
        for h in range(rows - 2):
            here = part_ref[f, h * columns : (h + 1) * columns]
            if h == 0:
                here = here + added[0][f]
            if h == rows - 3:
                here = here + added[1][f]
            here = here[:, 0:channels] + first_ref[f, h + 1][:, 0:channels].astype(F32)
            out_ref[f, h] = here.astype(BF16)
        pltpu.make_async_copy(out_ref.at[f], out_hbm.at[f], sems.at[f]).start()
    for f in range(frames):
        pltpu.make_async_copy(out_ref.at[f], out_hbm.at[f], sems.at[f]).wait()


def edges_of(pieces, channels):
    top = jnp.concatenate([p[:, :, :channels] for p in pieces], axis=2)
    bottom = jnp.concatenate([p[:, :, -channels:] for p in pieces], axis=2)
    return to_next(bottom), to_previous(top)


def shaped(shape, dtype):
    return jax.ShapeDtypeStruct(tuple(shape), dtype)


def window(
    latent,
    row_map,
    latent_cache,
    cache_one,
    cache_two,
    conv_in_w,
    weight_one,
    weight_two,
    gain_one,
    gain_two,
):
    frames, _, lc, columns = latent.shape
    tile_rows = latent_cache.shape[1]
    tiles, sources = lax.axis_size("tile"), lax.axis_size("src")
    channels = conv_in_w.shape[4]
    wide = channels * sources
    others = range(1, sources)

    taps = 27 * lc
    height = lc + -(-27 // GROUP) * lc + 16
    message = call(
        message_body,
        shaped((height, frames * columns), BF16),
        scratch=[
            pltpu.VMEM(latent.shape, BF16),
            pltpu.VMEM((1, channels), F32),
            pltpu.VMEM((1, channels), F32),
            pltpu.VMEM((taps, channels), BF16),
            pltpu.SemaphoreType.DMA((4,)),
        ],
        specs=[HBM] * 4,
    )(*stay(latent, gain_one[None], gain_two[None], conv_in_w.reshape(taps, channels)))
    got = xor_stage(message, "src", others)
    near = call(near_body, shaped((sources, lc, frames * columns), BF16), n_in=sources)(*got)
    for masks in far_masks(tiles):
        near = jnp.concatenate(xor_stage(near, "tile", masks), axis=0)
    far = xor_send(near, "tile", 1)

    caches = (cache_one.transpose(0, 1, 3, 2), cache_two.transpose(0, 1, 3, 2), latent_cache)
    strip = shaped((columns + 2 * lc, tile_rows * channels), BF16)
    rimmed = shaped((3, columns, tile_rows * channels), BF16)
    own_one, own_two, span, low, high = call(
        pack_body,
        (rimmed, rimmed, shaped((tile_rows, lc, 2 * columns), BF16), strip, strip),
        scratch=[pltpu.VMEM(x.shape, BF16) for x in caches] + [pltpu.SemaphoreType.DMA((3,))],
        specs=[HBM] * 3,
    )(*stay(*caches))
    before = to_next(high)
    after = to_previous(low)
    rim_one, rim_two = call(
        rim_body,
        (rimmed, rimmed),
        scratch=[pltpu.VMEM((2, columns, tile_rows * channels), BF16), pltpu.SemaphoreType.DMA((2,))],
        specs=[HBM, HBM, VMEM, VMEM],
        out_specs=(HBM, HBM),
        alias={0: 0, 1: 1},
    )(own_one, own_two, before, after)
    pieces_one = xor_stage(rim_one, "src", others)
    pieces_two = xor_stage(rim_two, "src", others)

    def turn(w):
        shape = shaped((9, wide, 256), BF16)
        return call(weights_body, (shape, shape), scratch=[pltpu.VMEM((3, wide, 128), F32)], n_in=1)(w)

    late_one, early_one = turn(weight_one)
    late_two, early_two = turn(weight_two)

    rows = tile_rows + 2
    spots = tile_rows * columns
    flops = 2 * 27 * wide * channels * spots

    def cached(pieces, early):
        return call(
            cached_body,
            shaped((2, spots, 128), F32),
            flops=flops,
            scratch=[pltpu.VMEM((2, rows, columns, 3 * wide), BF16)],
            n_in=5,
        )(*pieces, early)

    cached_one = cached(pieces_one, early_one)
    cached_two = cached(pieces_two, early_two)

    first, stat = call(
        first_body,
        (shaped((frames, rows, columns, wide), BF16), shaped((2, wide), F32)),
        flops=flops // 4,
        scratch=[
            pltpu.VMEM((rows + 2, frames + 2, 3 * lc, columns), BF16),
            pltpu.VMEM((27 * lc, wide), BF16),
            pltpu.SMEM((rows + 2,), jnp.int32),
        ],
        specs=[SMEM] + [VMEM] * 9,
    )(row_map, near, far, before, span, after, *got)

    def over_tiles(x):
        x = jnp.stack(xor_stage(x, "tile", [1]))
        stages = far_masks(tiles)
        for masks in stages[:-1]:
            x = jnp.concatenate(xor_stage(x, "tile", masks), axis=0)
        return xor_stage(x, "tile", stages[-1])

    count = frames * spots
    stats = over_tiles(stat)
    middle, stat_two = call(
        functools.partial(middle_body, len(stats), count),
        (shaped((frames, columns, tile_rows * channels), BF16), shaped((2, 128), F32)),
        flops=flops * 2,
        scratch=[
            pltpu.VMEM((frames, rows, columns, 3 * wide), BF16),
            pltpu.VMEM((frames, spots, 128), F32),
        ],
        n_in=len(stats) + 8,
    )(*stats, *got, first, cached_one, late_one, early_one)

    mids = xor_stage(middle, "src", others)
    stats = over_tiles(jnp.stack(xor_stage(stat_two, "src", others)))
    above, below = edges_of(mids, channels)
    part, scales = call(
        functools.partial(last_body, len(stats), count),
        (shaped((frames, spots, 128), F32), shaped((2, wide), F32)),
        flops=flops * 2,
        scratch=[pltpu.VMEM((frames, rows, columns, 3 * wide), BF16)],
        n_in=len(stats) + 11,
    )(*stats, *got, *mids, cached_two, late_two, early_two)
    decoded = call(
        edge_body,
        shaped((frames, tile_rows, columns, channels), BF16),
        flops=flops // 2,
        scratch=[
            pltpu.VMEM((frames, 2, columns, 3 * wide), BF16),
            pltpu.VMEM((frames, tile_rows, columns, channels), BF16),
            pltpu.SemaphoreType.DMA((frames,)),
        ],
        n_in=7,
        out_specs=HBM,
    )(part, scales, above, below, first, late_two, early_two)
    return decoded.transpose(0, 1, 3, 2)


def solution(mesh):
    placed = (
        P(None, ("src", "tile"), None, None),
        P(),
        P(None, "tile", None, None),
        P(None, "tile", "src", None),
        P(None, "tile", "src", None),
        P(None, None, None, None, "src"),
        P(None, None, None, "src", None),
        P(None, None, None, "src", None),
        P("src"),
        P("src"),
    )
    return jax.shard_map(
        window,
        mesh=mesh,
        in_specs=placed,
        out_specs=P(None, "tile", "src", None),
        check_vma=False,
    )
```

```python
import functools

import jax
import jax.numpy as jnp
from jax import lax
from jax.experimental import pallas as pl
from jax.experimental.pallas import tpu as pltpu
from jax.sharding import PartitionSpec as P


GSIZE = 12
F32 = jnp.float32
BF16 = jnp.bfloat16
VMEM_LIMIT = 24 << 20
VMEM = pl.BlockSpec(memory_space=pltpu.VMEM)
SMEM = pl.BlockSpec(memory_space=pltpu.SMEM)
HBM = pl.BlockSpec(memory_space=pl.ANY)


def call(body, outs, flops=0, scratch=(), specs=None, n_in=0, out_specs=None, limit=VMEM_LIMIT, alias=None):
    return pl.pallas_call(
        body,
        out_shape=outs,
        in_specs=specs if specs is not None else [VMEM] * n_in,
        out_specs=out_specs if out_specs is not None else jax.tree.map(lambda _: VMEM, outs),
        scratch_shapes=list(scratch),
        input_output_aliases=alias or {},
        cost_estimate=pl.CostEstimate(flops=flops, bytes_accessed=1 << 20, transcendentals=0),
        compiler_params=pltpu.CompilerParams(vmem_limit_bytes=limit),
    )


def xor_send(x, axis, mask):
    return lax.ppermute(x, axis, [(i, i ^ mask) for i in range(lax.axis_size(axis))])


def xor_stage(x, axis, masks):
    return [x] + [xor_send(x, axis, m) for m in masks]


def far_masks(size):
    low, stages = 2, []
    while low < size:
        if low * 2 < size:
            stages.append([low, 2 * low, 3 * low])
            low *= 4
        else:
            stages.append([low])
            low *= 2
    return stages


def stay(*arrays):
    return [pltpu.with_memory_space_constraint(x, pltpu.HBM) for x in arrays]


def to_next(x):
    return lax.ppermute(x, "tile", [(i, i + 1) for i in range(lax.axis_size("tile") - 1)])


def to_previous(x):
    return lax.ppermute(x, "tile", [(i + 1, i) for i in range(lax.axis_size("tile") - 1)])


def fetch(sources, targets, sems):
    copies = [pltpu.make_async_copy(src, dst, sems.at[n]) for n, (src, dst) in enumerate(zip(sources, targets))]
    for copy in copies:
        copy.start()
    for copy in copies:
        copy.wait()


GROUP = 5


def message_body(*refs):
    out_ref, latent_ref, gain_a, gain_b, w_ref, sems = refs[4:]
    fetch(refs[:4], (latent_ref, gain_a, gain_b, w_ref), sems)
    lc, channels = latent_ref.shape[2], gain_a.shape[1]

    def joined(parts):
        return jnp.concatenate([part.astype(F32) for part in parts], axis=1).astype(BF16)

    out_ref[0:lc, :] = joined([latent_ref[f, 0] for f in range(latent_ref.shape[0])])
    taps = w_ref.shape[0] // lc
    for n in range(0, taps, GROUP):
        held = [w_ref[k * lc : (k + 1) * lc] for k in range(n, min(n + GROUP, taps))]
        at = lc + n // GROUP * lc
        out_ref[at : at + lc, 0 : len(held) * channels] = joined(held)
    gains = jnp.concatenate([gain_a[...], gain_b[...]], axis=1)
    at = out_ref.shape[0] - 16
    terms = []
    for _ in range(3):
        terms.append(gains.astype(BF16).astype(F32))
        gains = gains - terms[-1]
    rows = jnp.concatenate(terms + [jnp.zeros((13, gains.shape[1]), F32)], axis=0)
    out_ref[at:, 0 : gains.shape[1]] = rows.astype(BF16)


def near_body(*refs):
    out_ref = refs[-1]
    for n, ref in enumerate(refs[:-1]):
        out_ref[n] = ref[0 : out_ref.shape[1], :]


def pack_body(*refs):
    own_one, own_two, span_out, low_ref, high_ref, *here, sems = refs[3:]
    fetch(refs[:3], here, sems)
    one_ref, two_ref, span_ref = here
    frames, rows = one_ref.shape[0], one_ref.shape[1]
    columns, lc = one_ref.shape[2], span_ref.shape[2]

    def joined(parts):
        return jnp.concatenate([part.astype(F32) for part in parts], axis=1).astype(BF16)

    for ref, out in ((one_ref, own_one), (two_ref, own_two)):
        for f in range(frames):
            out[f] = joined([ref[f, h] for h in range(rows)])
    every = [ref.at[f] for ref in (one_ref, two_ref) for f in range(frames)]
    low_ref[0:columns, :] = joined([ref[0] for ref in every])
    high_ref[0:columns, :] = joined([ref[rows - 1] for ref in every])
    width = span_ref.shape[3] * frames
    for ref in (low_ref, high_ref):
        ref[columns:, :] = jnp.zeros_like(ref[columns:, :])
    for row in range(rows):
        both = joined([span_ref[f, row] for f in range(frames)])
        span_out[row] = both
        if row < 2:
            low_ref[columns + row * lc : columns + (row + 1) * lc, 0:width] = both
        if row >= rows - 2:
            at = columns + (row - rows + 2) * lc
            high_ref[at : at + lc, 0:width] = both


def rim_body(one_in, two_in, before, after, one_out, two_out, held, sems):
    columns = held.shape[1]
    channels = held.shape[2] // 4
    copies = []
    for n, out in enumerate((one_out, two_out)):
        parts = []
        for f in range(2):
            lanes = slice((2 * n + f) * channels, (2 * n + f + 1) * channels)
            parts += [side[0:columns, lanes].astype(F32) for side in (before, after)]
        held[n] = jnp.concatenate(parts, axis=1).astype(BF16)
        copies.append(pltpu.make_async_copy(held.at[n], out.at[2], sems.at[n]))
        copies[-1].start()
    for copy in copies:
        copy.wait()


def weights_body(w_ref, late_ref, early_ref, turned):
    outs, ins = w_ref.shape[3], w_ref.shape[4]
    mine = lax.axis_index("src")
    turned[...] = jnp.zeros_like(turned)

    def tap(n, _):
        b, e = n // 3, n % 3
        for a in range(3):
            turned[a, :, 0:outs] = w_ref[a, b, e].T
        for slot in range(ins // outs):
            start = pl.multiple_of(jnp.bitwise_xor(mine, slot) * outs, 16)
            here = pl.ds(slot * outs, outs)
            early, middle, late = [turned[a, pl.ds(start, outs), :] for a in range(3)]
            late_ref[n, here, 0:128] = late
            late_ref[n, here, 128:256] = middle
            early_ref[n, here, 0:128] = middle
            early_ref[n, here, 128:256] = early
        return 0

    lax.fori_loop(0, 9, tap, 0)


def first_body(map_ref, near_ref, far_ref, before, own, after, m0, m1, m2, m3, first_ref, stat_ref, taps, wall, tab_ref):
    half = near_ref.shape[0]
    rows = own.shape[0] + 4
    columns = own.shape[2] // 2
    frames = near_ref.shape[2] // columns
    s, t, tiles = lax.axis_index("src"), lax.axis_index("tile"), lax.axis_size("tile")
    top = t * (rows - 4) - 2
    for row in range(rows):
        tab_ref[row] = -1
    for i in range(map_ref.shape[0]):
        at = map_ref[i] - top
        to_t, to_s = jnp.bitwise_xor(i % tiles, t), jnp.bitwise_xor(i // tiles, s)
        place = to_t % 2 * half + to_t // 2 * 4 + to_s

        @pl.when(jnp.logical_and(at >= 0, at < rows))
        def _():
            tab_ref[jnp.clip(at, 0, rows - 1)] = place

    wide = wall.shape[1]
    for n in range(wall.shape[0] // 16):
        at, lanes = 16 + n // GROUP * 16, slice(n % GROUP * wide // 4, (n % GROUP + 1) * wide // 4)
        parts = [m[at : at + 16, lanes].astype(F32) for m in (m0, m1, m2, m3)]
        a, b, e = n // 9, n // 3 % 3, n % 3
        put = 16 * (9 * b + 3 * a + e)
        wall[put : put + 16, :] = jnp.concatenate(parts, axis=1).astype(BF16)
    for row in range(rows):
        place = tab_ref[row]
        kept = (place >= 0).astype(F32)
        inner = jnp.maximum(jnp.where(place >= half, place - half, place), 0)
        new = jnp.where(place >= half, far_ref[inner].astype(F32), near_ref[inner].astype(F32)) * kept
        if 2 <= row < rows - 2:
            old = own[row - 2].astype(F32)
        else:
            at = columns + 16 * (row if row < 2 else row - rows + 2)
            old = (before if row < 2 else after)[at : at + 16, 0 : 2 * columns].astype(F32)
        line = [old[:, f * columns : (f + 1) * columns] for f in range(2)]
        line += [new[:, f * columns : (f + 1) * columns] for f in range(frames)]
        v = jnp.concatenate(line, axis=0)
        zero = jnp.zeros((v.shape[0], 1), F32)
        left = jnp.concatenate([zero, v[:, : columns - 1]], axis=1)
        right = jnp.concatenate([v[:, 1:], zero], axis=1)
        parts = [x[16 * f : 16 * f + 16] for f in range(frames + 2) for x in (left, v, right)]
        taps[row] = jnp.concatenate(parts, axis=0).astype(BF16).T
    total = jnp.zeros((8, wall.shape[1]), F32)
    for t in range(frames):
        for r in range(rows - 2):
            patch = jnp.concatenate([taps[r + b, :, 48 * t : 48 * t + 144] for b in range(3)], axis=1)
            got = jnp.dot(patch, wall[...], preferred_element_type=F32).astype(BF16)
            first_ref[t, r] = got
            if 0 < r < rows - 3:
                total += jnp.sum(got.astype(F32).reshape(columns // 8, 8, -1), axis=0)
    count = frames * (rows - 4) * columns
    mean = jnp.sum(total, axis=0, keepdims=True) * (1.0 / count)
    square = jnp.zeros((8, wall.shape[1]), F32)
    for t in range(frames):
        for r in range(1, rows - 3):
            d = first_ref[t, r].astype(F32) - mean
            square += jnp.sum((d * d).reshape(columns // 8, 8, -1), axis=0)
    stat_ref[0:1, :] = mean
    stat_ref[1:2, :] = jnp.sum(square, axis=0, keepdims=True)


def scale_shift(means, squares, gain, count):
    channels = gain.shape[1]
    lane = lax.broadcasted_iota(jnp.int32, (channels, channels), 0) // GSIZE
    other = lax.broadcasted_iota(jnp.int32, (channels, channels), 1) // GSIZE
    same = (lane == other).astype(F32)

    def over_group(v):
        v = jnp.broadcast_to(v, (8, channels))
        return jnp.dot(v, same, precision=lax.Precision.HIGHEST, preferred_element_type=F32)[0:1]

    tiles = sum(m.shape[0] for m in means)
    mean = over_group(sum(jnp.sum(m, axis=0, keepdims=True) for m in means)) * (1.0 / (tiles * GSIZE))
    spread = jnp.zeros_like(mean)
    for m, q in zip(means, squares):
        spread += jnp.sum(q + float(count) * (m - mean) * (m - mean), axis=0, keepdims=True)
    variance = over_group(spread) * (1.0 / (count * tiles * GSIZE))
    scale = lax.rsqrt(variance + 1e-06) * gain
    return mean, scale


def put_row(taps, f, r, v):
    columns, channels = v.shape
    at = lax.broadcasted_iota(jnp.int32, v.shape, 0)
    left = jnp.where(at == 0, 0.0, pltpu.roll(v, 1, axis=0))
    right = jnp.where(at == columns - 1, 0.0, pltpu.roll(v, columns - 1, axis=0))
    taps[f, r, :, 0:channels] = left.astype(BF16)
    taps[f, r, :, channels : 2 * channels] = v.astype(BF16)
    taps[f, r, :, 2 * channels :] = right.astype(BF16)


def activate(v, mean, scale):
    y = (v - mean) * scale
    return (0.5 * y) * (1.0 + jnp.tanh(0.5 * y))


def row_sum(got, columns, inner):
    if not inner:
        return got[0] + got[1] + got[2]
    above, here, below = got
    head = here[:columns] + below[:columns]
    tail = here[-columns:] + above[-columns:]
    return jnp.concatenate([head, here[columns:-columns] + above[:-columns] + below[columns:], tail], axis=0)


def row_span(b, rows, inner):
    return (max(1, b), min(rows - 1, b + rows - 2)) if inner else (b, b + rows - 2)


def tap_product(taps, f, w_ref, lanes, inner=False):
    _, rows, columns, depth = taps.shape
    got = []
    for b in range(3):
        first, end = row_span(b, rows, inner)
        x = taps[f, first:end].reshape((end - first) * columns, depth)
        w = w_ref[3 * b : 3 * b + 3, :, lanes].reshape(depth, lanes.stop - lanes.start)
        got.append(jnp.dot(x, w, preferred_element_type=F32))
    return row_sum(got, columns, inner)


def lone_product(taps, f, w_ref, lanes, inner=False):
    _, rows, columns, depth = taps.shape
    depth //= 3
    outer, centre = [], []
    if not inner:
        x = [taps[f, b : b + rows - 2, :, depth : 2 * depth].reshape((rows - 2) * columns, depth) for b in range(3)]
        x = jnp.concatenate(x, axis=1)
        w = [jnp.concatenate([w_ref[3 * b + e, :, lanes] for b in range(3)], axis=0) for e in range(3)]
        outer = [jnp.dot(x, jnp.concatenate([w[0], w[2]], axis=1), preferred_element_type=F32), 0.0, 0.0]
        centre = [jnp.dot(x, w[1], preferred_element_type=F32), 0.0, 0.0]
    for b in range(0 if not inner else 3):
        first, end = row_span(b, rows, inner)
        x = taps[f, first:end, :, depth : 2 * depth].reshape((end - first) * columns, depth)
        pair = jnp.concatenate([w_ref[3 * b, :, lanes], w_ref[3 * b + 2, :, lanes]], axis=1)
        outer.append(jnp.dot(x, pair, preferred_element_type=F32))
        centre.append(jnp.dot(x, w_ref[3 * b + 1, :, lanes], preferred_element_type=F32))
    outer, centre = row_sum(outer, columns, inner), row_sum(centre, columns, inner)
    left, right = outer[:, 0:128], outer[:, 128:256]
    at = lax.broadcasted_iota(jnp.int32, left.shape, 0) % columns
    left = jnp.where(at == 0, 0.0, pltpu.roll(left, 1, axis=0))
    right = jnp.where(at == columns - 1, 0.0, pltpu.roll(right, left.shape[0] - 1, axis=0))
    return centre + left + right


def spread_rows(own, up, down, f, r, rows, channels):
    if r == 0:
        return up[f].astype(F32)
    if r == rows - 1:
        return down[f].astype(F32)
    lanes = slice((r - 1) * channels, r * channels)
    return jnp.concatenate([piece[f, :, lanes].astype(F32) for piece in own], axis=1)


def cached_body(p0, p1, p2, p3, early_ref, out_ref, taps):
    pieces = (p0, p1, p2, p3)
    rows = taps.shape[1]
    channels = p0.shape[2] // (rows - 2)
    for f in range(2):
        for r in range(rows):
            if 0 < r < rows - 1:
                v = spread_rows(pieces, None, None, f, r, rows, channels)
            else:
                at = (2 * f + (r > 0)) * channels
                v = jnp.concatenate([piece[2, :, at : at + channels].astype(F32) for piece in pieces], axis=1)
            put_row(taps, f, r, v)
    one = lone_product(taps, 0, early_ref, slice(128, 256))
    both = tap_product(taps, 1, early_ref, slice(0, 256))
    out_ref[0] = one + both[:, 0:128]
    out_ref[1] = both[:, 128:256]


def conv_current(taps, late_ref, early_ref, cached_ref, inner=False):
    both = tap_product(taps, 0, late_ref, slice(0, 256), inner)
    yield cached_ref[0] + both[:, 0:128]
    middle = cached_ref[1] + both[:, 128:256]
    last = lone_product(taps, 0, early_ref, slice(128, 256), inner)
    both = tap_product(taps, 1, late_ref, slice(0, 256), inner)
    yield middle + both[:, 0:128]
    last = last + both[:, 128:256]
    yield last + lone_product(taps, 2, late_ref, slice(0, 128), inner)


def gain_of(refs, n, channels):
    at = refs[0].shape[0] - 16
    lanes = slice(n * channels, (n + 1) * channels)
    terms = [ref[at : at + 16, lanes].astype(F32) for ref in refs]
    return jnp.concatenate([(t[0:1] + t[1:2]) + t[2:3] for t in terms], axis=1)


def inside():
    t = lax.axis_index("tile")
    return (t > 0).astype(F32), (t < lax.axis_size("tile") - 1).astype(F32)


def middle_body(n_stats, count, *refs):
    stats = refs[:n_stats]
    gains = refs[n_stats : n_stats + 4]
    first_ref, cached_ref, late_ref, early_ref, out_ref, stat_ref, taps, kept = refs[n_stats + 4 :]
    edges = inside()
    means = [s[:, 0, :] for s in stats]
    squares = [s[:, 1, :] for s in stats]
    mean, scale = scale_shift(means, squares, gain_of(gains, 0, first_ref.shape[3] // 4), count)
    frames, rows, columns, _ = taps.shape
    for f in range(frames):
        for r in range(rows):
            v = activate(first_ref[f, r].astype(F32), mean, scale)
            if r == 0:
                v = v * edges[0]
            if r == rows - 1:
                v = v * edges[1]
            put_row(taps, f, r, v)
    channels = out_ref.shape[2] // (rows - 2)
    total = jnp.zeros((1, 128), F32)
    for f, got in enumerate(conv_current(taps, late_ref, early_ref, cached_ref)):
        kept[f] = got
        total += jnp.sum(got, axis=0, keepdims=True)
        parts = [got[h * columns : (h + 1) * columns, 0:channels] for h in range(rows - 2)]
        out_ref[f] = jnp.concatenate(parts, axis=1).astype(BF16)
    local = total * (1.0 / (frames * (rows - 2) * columns))
    square = jnp.zeros((1, 128), F32)
    for f in range(frames):
        d = kept[f] - local
        square += jnp.sum(d * d, axis=0, keepdims=True)
    stat_ref[0:1, :] = local
    stat_ref[1:2, :] = square


def last_body(n_stats, count, *refs):
    stats = refs[:n_stats]
    gains, (p0, p1, p2, *p3) = refs[n_stats : n_stats + 4], refs[n_stats + 4 : n_stats + 9]
    cached_ref, late_ref, early_ref, out_ref, scale_ref, taps = refs[n_stats + 9 :]
    frames, rows, _, _ = taps.shape
    channels = p0.shape[2] // (rows - 2)

    def wide(s, n):
        return jnp.concatenate([s[:, slot, n, 0:channels] for slot in range(4)], axis=1)

    means = [wide(s, 0) for s in stats]
    squares = [wide(s, 1) for s in stats]
    mean, scale = scale_shift(means, squares, gain_of(gains, 1, channels), count)
    scale_ref[0:1, :] = mean
    scale_ref[1:2, :] = scale
    for f in range(frames):
        for r in range(1, rows - 1):
            at = slice((r - 1) * channels, r * channels)
            far = jnp.concatenate([piece[f, :, at].astype(F32) for piece in p3], axis=0)
            v = jnp.concatenate([piece[f, :, at].astype(F32) for piece in (p0, p1, p2)] + [far], axis=1)
            put_row(taps, f, r, activate(v, mean, scale))
    for f, got in enumerate(conv_current(taps, late_ref, early_ref, cached_ref, True)):
        out_ref[f] = got


def edge_body(part_ref, scale_ref, up, down, first_ref, late_ref, early_ref, out_hbm, taps, out_ref, sems):
    frames, _, columns, depth = taps.shape
    rows = first_ref.shape[1]
    channels = out_ref.shape[3]
    mean, scale = scale_ref[0:1, :], scale_ref[1:2, :]
    added = []
    for side, (ref, kept, b) in enumerate(zip((up, down), inside(), (0, 2))):
        for f in range(frames):
            put_row(taps, f, side, activate(ref[f].astype(F32), mean, scale) * kept)
        taken = slice(3 * b, 3 * b + 3)
        x = jnp.concatenate([taps[f, side] for f in range(frames)], axis=0)
        both = jnp.dot(x, late_ref[taken].reshape(depth, 256), preferred_element_type=F32)
        late = jnp.dot(taps[0, side], early_ref[taken, :, 128:256].reshape(depth, 128), preferred_element_type=F32)
        now, then = both[:, 0:128], both[:, 128:256]
        added.append(
            [
                now[0:columns],
                now[columns : 2 * columns] + then[0:columns],
                now[2 * columns :] + then[columns : 2 * columns] + late,
            ]
        )
    for f in range(frames):
        for h in range(rows - 2):
            here = part_ref[f, h * columns : (h + 1) * columns]
            if h == 0:
                here = here + added[0][f]
            if h == rows - 3:
                here = here + added[1][f]
            here = here[:, 0:channels] + first_ref[f, h + 1][:, 0:channels].astype(F32)
            out_ref[f, h] = here.astype(BF16)
        pltpu.make_async_copy(out_ref.at[f], out_hbm.at[f], sems.at[f]).start()
    for f in range(frames):
        pltpu.make_async_copy(out_ref.at[f], out_hbm.at[f], sems.at[f]).wait()


def edges_of(pieces, channels):
    top = jnp.concatenate([p[:, :, :channels] for p in pieces], axis=2)
    bottom = jnp.concatenate([p[:, :, -channels:] for p in pieces], axis=2)
    return to_next(bottom), to_previous(top)


def shaped(shape, dtype):
    return jax.ShapeDtypeStruct(tuple(shape), dtype)


def window(
    latent,
    row_map,
    latent_cache,
    cache_one,
    cache_two,
    conv_in_w,
    weight_one,
    weight_two,
    gain_one,
    gain_two,
):
    frames, _, lc, columns = latent.shape
    tile_rows = latent_cache.shape[1]
    tiles, sources = lax.axis_size("tile"), lax.axis_size("src")
    channels = conv_in_w.shape[4]
    wide = channels * sources
    others = range(1, sources)

    taps = 27 * lc
    height = lc + -(-27 // GROUP) * lc + 16
    message = call(
        message_body,
        shaped((height, frames * columns), BF16),
        scratch=[
            pltpu.VMEM(latent.shape, BF16),
            pltpu.VMEM((1, channels), F32),
            pltpu.VMEM((1, channels), F32),
            pltpu.VMEM((taps, channels), BF16),
            pltpu.SemaphoreType.DMA((4,)),
        ],
        specs=[HBM] * 4,
    )(*stay(latent, gain_one[None], gain_two[None], conv_in_w.reshape(taps, channels)))
    got = xor_stage(message, "src", others)
    near = call(near_body, shaped((sources, lc, frames * columns), BF16), n_in=sources)(*got)
    for masks in far_masks(tiles):
        near = jnp.concatenate(xor_stage(near, "tile", masks), axis=0)
    far = xor_send(near, "tile", 1)

    caches = (cache_one.transpose(0, 1, 3, 2), cache_two.transpose(0, 1, 3, 2), latent_cache)
    strip = shaped((columns + 2 * lc, tile_rows * channels), BF16)
    rimmed = shaped((3, columns, tile_rows * channels), BF16)
    own_one, own_two, span, low, high = call(
        pack_body,
        (rimmed, rimmed, shaped((tile_rows, lc, 2 * columns), BF16), strip, strip),
        scratch=[pltpu.VMEM(x.shape, BF16) for x in caches] + [pltpu.SemaphoreType.DMA((3,))],
        specs=[HBM] * 3,
    )(*stay(*caches))
    before = to_next(high)
    after = to_previous(low)
    rim_one, rim_two = call(
        rim_body,
        (rimmed, rimmed),
        scratch=[pltpu.VMEM((2, columns, tile_rows * channels), BF16), pltpu.SemaphoreType.DMA((2,))],
        specs=[HBM, HBM, VMEM, VMEM],
        out_specs=(HBM, HBM),
        alias={0: 0, 1: 1},
    )(own_one, own_two, before, after)
    pieces_one = xor_stage(rim_one, "src", others)
    pieces_two = xor_stage(rim_two, "src", others)

    def turn(w):
        shape = shaped((9, wide, 256), BF16)
        return call(weights_body, (shape, shape), scratch=[pltpu.VMEM((3, wide, 128), BF16)], n_in=1)(w)

    late_one, early_one = turn(weight_one)
    late_two, early_two = turn(weight_two)

    rows = tile_rows + 2
    spots = tile_rows * columns
    flops = 2 * 27 * wide * channels * spots

    def cached(pieces, early):
        return call(
            cached_body,
            shaped((2, spots, 128), F32),
            flops=flops,
            scratch=[pltpu.VMEM((2, rows, columns, 3 * wide), BF16)],
            n_in=5,
        )(*pieces, early)

    cached_one = cached(pieces_one, early_one)
    cached_two = cached(pieces_two, early_two)

    first, stat = call(
        first_body,
        (shaped((frames, rows, columns, wide), BF16), shaped((2, wide), F32)),
        flops=flops // 4,
        scratch=[
            pltpu.VMEM((rows + 2, columns, (frames + 2) * 3 * lc), BF16),
            pltpu.VMEM((27 * lc, wide), BF16),
            pltpu.SMEM((rows + 2,), jnp.int32),
        ],
        specs=[SMEM] + [VMEM] * 9,
    )(row_map, near, far, before, span, after, *got)

    def over_tiles(x, stages):
        x = jnp.stack(xor_stage(x, "tile", [1]))
        for masks in stages[:-1]:
            x = jnp.concatenate(xor_stage(x, "tile", masks), axis=0)
        return xor_stage(x, "tile", stages[-1])

    doubling = [[1 << n] for n in range(1, tiles.bit_length() - 1)]
    count = frames * spots
    stats = over_tiles(stat, doubling)
    middle, stat_two = call(
        functools.partial(middle_body, len(stats), count),
        (shaped((frames, columns, tile_rows * channels), BF16), shaped((2, 128), F32)),
        flops=flops * 2,
        scratch=[
            pltpu.VMEM((frames, rows, columns, 3 * wide), BF16),
            pltpu.VMEM((frames, spots, 128), F32),
        ],
        n_in=len(stats) + 8,
    )(*stats, *got, first, cached_one, late_one, early_one)

    mids = xor_stage(middle, "src", [1, 2])
    cut = columns // 2
    mids += [xor_send(mids[1][:, :cut], "src", 2), xor_send(mids[2][:, cut:], "src", 1)]
    stats = over_tiles(jnp.stack(xor_stage(stat_two, "src", others)), far_masks(tiles))
    above, below = edges_of(mids[:3] + [jnp.concatenate(mids[3:], axis=1)], channels)
    part, scales = call(
        functools.partial(last_body, len(stats), count),
        (shaped((frames, spots, 128), F32), shaped((2, wide), F32)),
        flops=flops * 2,
        scratch=[pltpu.VMEM((frames, rows, columns, 3 * wide), BF16)],
        n_in=len(stats) + 12,
    )(*stats, *got, *mids, cached_two, late_two, early_two)
    decoded = call(
        edge_body,
        shaped((frames, tile_rows, columns, channels), BF16),
        flops=flops // 2,
        scratch=[
            pltpu.VMEM((frames, 2, columns, 3 * wide), BF16),
            pltpu.VMEM((frames, tile_rows, columns, channels), BF16),
            pltpu.SemaphoreType.DMA((frames,)),
        ],
        n_in=7,
        out_specs=HBM,
    )(part, scales, above, below, first, late_two, early_two)
    return decoded.transpose(0, 1, 3, 2)


def solution(mesh):
    placed = (
        P(None, ("src", "tile"), None, None),
        P(),
        P(None, "tile", None, None),
        P(None, "tile", "src", None),
        P(None, "tile", "src", None),
        P(None, None, None, None, "src"),
        P(None, None, None, "src", None),
        P(None, None, None, "src", None),
        P("src"),
        P("src"),
    )
    return jax.shard_map(
        window,
        mesh=mesh,
        in_specs=placed,
        out_specs=P(None, "tile", "src", None),
        check_vma=False,
    )
```

```python
import functools

import jax
import jax.numpy as jnp
from jax import lax
from jax.experimental import pallas as pl
from jax.experimental.pallas import tpu as pltpu
from jax.sharding import PartitionSpec as P


GSIZE = 12
F32 = jnp.float32
BF16 = jnp.bfloat16
VMEM_LIMIT = 24 << 20
VMEM = pl.BlockSpec(memory_space=pltpu.VMEM)
SMEM = pl.BlockSpec(memory_space=pltpu.SMEM)
HBM = pl.BlockSpec(memory_space=pl.ANY)


def call(body, outs, flops=0, scratch=(), specs=None, n_in=0, out_specs=None, limit=VMEM_LIMIT, alias=None):
    return pl.pallas_call(
        body,
        out_shape=outs,
        in_specs=specs if specs is not None else [VMEM] * n_in,
        out_specs=out_specs if out_specs is not None else jax.tree.map(lambda _: VMEM, outs),
        scratch_shapes=list(scratch),
        input_output_aliases=alias or {},
        cost_estimate=pl.CostEstimate(flops=flops, bytes_accessed=1 << 20, transcendentals=0),
        compiler_params=pltpu.CompilerParams(vmem_limit_bytes=limit),
    )


def xor_send(x, axis, mask):
    return lax.ppermute(x, axis, [(i, i ^ mask) for i in range(lax.axis_size(axis))])


def xor_stage(x, axis, masks):
    return [x] + [xor_send(x, axis, m) for m in masks]


def far_masks(size):
    low, stages = 2, []
    while low < size:
        if low * 2 < size:
            stages.append([low, 2 * low, 3 * low])
            low *= 4
        else:
            stages.append([low])
            low *= 2
    return stages


def stay(*arrays):
    return [pltpu.with_memory_space_constraint(x, pltpu.HBM) for x in arrays]


def to_next(x):
    return lax.ppermute(x, "tile", [(i, i + 1) for i in range(lax.axis_size("tile") - 1)])


def to_previous(x):
    return lax.ppermute(x, "tile", [(i + 1, i) for i in range(lax.axis_size("tile") - 1)])


def fetch(sources, targets, sems):
    copies = [pltpu.make_async_copy(src, dst, sems.at[n]) for n, (src, dst) in enumerate(zip(sources, targets))]
    for copy in copies:
        copy.start()
    for copy in copies:
        copy.wait()


GROUP = 5


def message_body(*refs):
    out_ref, latent_ref, gain_a, gain_b, w_ref, sems = refs[4:]
    fetch(refs[:4], (latent_ref, gain_a, gain_b, w_ref), sems)
    lc, channels = latent_ref.shape[2], gain_a.shape[1]

    def joined(parts):
        return jnp.concatenate([part.astype(F32) for part in parts], axis=1).astype(BF16)

    out_ref[0:lc, :] = joined([latent_ref[f, 0] for f in range(latent_ref.shape[0])])
    taps = w_ref.shape[0] // lc
    for n in range(0, taps, GROUP):
        held = [w_ref[k * lc : (k + 1) * lc] for k in range(n, min(n + GROUP, taps))]
        at = lc + n // GROUP * lc
        out_ref[at : at + lc, 0 : len(held) * channels] = joined(held)
    gains = jnp.concatenate([gain_a[...], gain_b[...]], axis=1)
    at = out_ref.shape[0] - 16
    terms = []
    for _ in range(3):
        terms.append(gains.astype(BF16).astype(F32))
        gains = gains - terms[-1]
    rows = jnp.concatenate(terms + [jnp.zeros((13, gains.shape[1]), F32)], axis=0)
    lane = taps % GROUP * channels
    out_ref[at:, lane : lane + gains.shape[1]] = rows.astype(BF16)


def near_body(*refs):
    out_ref = refs[-1]
    for n, ref in enumerate(refs[:-1]):
        out_ref[n] = ref[0 : out_ref.shape[1], :]


def pack_body(*refs):
    own_one, own_two, span_out, low_ref, high_ref, *here, sems = refs[3:]
    fetch(refs[:3], here, sems)
    one_ref, two_ref, span_ref = here
    frames, rows = one_ref.shape[0], one_ref.shape[1]
    columns, lc = one_ref.shape[2], span_ref.shape[2]

    def joined(parts):
        return jnp.concatenate([part.astype(F32) for part in parts], axis=1).astype(BF16)

    for ref, out in ((one_ref, own_one), (two_ref, own_two)):
        for f in range(frames):
            out[f] = joined([ref[f, h] for h in range(rows)])
    every = [ref.at[f] for ref in (one_ref, two_ref) for f in range(frames)]
    low_ref[0:columns, :] = joined([ref[0] for ref in every])
    high_ref[0:columns, :] = joined([ref[rows - 1] for ref in every])
    width = span_ref.shape[3] * frames
    for ref in (low_ref, high_ref):
        ref[columns:, :] = jnp.zeros_like(ref[columns:, :])
    for row in range(rows):
        both = joined([span_ref[f, row] for f in range(frames)])
        span_out[row] = both
        if row < 2:
            low_ref[columns + row * lc : columns + (row + 1) * lc, 0:width] = both
        if row >= rows - 2:
            at = columns + (row - rows + 2) * lc
            high_ref[at : at + lc, 0:width] = both


def rim_body(one_in, two_in, before, after, one_out, two_out, held, sems):
    columns = held.shape[1]
    channels = held.shape[2] // 4
    copies = []
    for n, out in enumerate((one_out, two_out)):
        parts = []
        for f in range(2):
            lanes = slice((2 * n + f) * channels, (2 * n + f + 1) * channels)
            parts += [side[0:columns, lanes].astype(F32) for side in (before, after)]
        held[n] = jnp.concatenate(parts, axis=1).astype(BF16)
        copies.append(pltpu.make_async_copy(held.at[n], out.at[2], sems.at[n]))
        copies[-1].start()
    for copy in copies:
        copy.wait()


def weights_body(w_ref, late_ref, early_ref, turned):
    outs, ins = w_ref.shape[3], w_ref.shape[4]
    mine = lax.axis_index("src")
    turned[...] = jnp.zeros_like(turned)

    def tap(n, _):
        b, e = n // 3, n % 3
        for a in range(3):
            turned[a, :, 0:outs] = w_ref[a, b, e].T
        for slot in range(ins // outs):
            start = pl.multiple_of(jnp.bitwise_xor(mine, slot) * outs, 16)
            here = pl.ds(slot * outs, outs)
            early, middle, late = [turned[a, pl.ds(start, outs), :] for a in range(3)]
            late_ref[n, here, 0:128] = late
            late_ref[n, here, 128:256] = middle
            early_ref[n, here, 0:128] = middle
            early_ref[n, here, 128:256] = early
        return 0

    lax.fori_loop(0, 9, tap, 0)


def first_body(map_ref, near_ref, far_ref, before, own, after, m0, m1, m2, m3, first_ref, stat_ref, taps, wall, tab_ref):
    half = near_ref.shape[0]
    rows = own.shape[0] + 4
    columns = own.shape[2] // 2
    frames = near_ref.shape[2] // columns
    s, t, tiles = lax.axis_index("src"), lax.axis_index("tile"), lax.axis_size("tile")
    top = t * (rows - 4) - 2
    for row in range(rows):
        tab_ref[row] = -1
    for i in range(map_ref.shape[0]):
        at = map_ref[i] - top
        to_t, to_s = jnp.bitwise_xor(i % tiles, t), jnp.bitwise_xor(i // tiles, s)
        place = to_t % 2 * half + to_t // 2 * 4 + to_s

        @pl.when(jnp.logical_and(at >= 0, at < rows))
        def _():
            tab_ref[jnp.clip(at, 0, rows - 1)] = place

    wide = wall.shape[1]
    for n in range(wall.shape[0] // 16):
        at, lanes = 16 + n // GROUP * 16, slice(n % GROUP * wide // 4, (n % GROUP + 1) * wide // 4)
        parts = [m[at : at + 16, lanes].astype(F32) for m in (m0, m1, m2, m3)]
        a, b, e = n // 9, n // 3 % 3, n % 3
        put = 16 * (9 * b + 3 * a + e)
        wall[put : put + 16, :] = jnp.concatenate(parts, axis=1).astype(BF16)
    for row in range(rows):
        place = tab_ref[row]
        kept = (place >= 0).astype(F32)
        inner = jnp.maximum(jnp.where(place >= half, place - half, place), 0)
        new = jnp.where(place >= half, far_ref[inner].astype(F32), near_ref[inner].astype(F32)) * kept
        if 2 <= row < rows - 2:
            old = own[row - 2].astype(F32)
        else:
            at = columns + 16 * (row if row < 2 else row - rows + 2)
            old = (before if row < 2 else after)[at : at + 16, 0 : 2 * columns].astype(F32)
        line = [old[:, f * columns : (f + 1) * columns] for f in range(2)]
        line += [new[:, f * columns : (f + 1) * columns] for f in range(frames)]
        v = jnp.concatenate(line, axis=0)
        zero = jnp.zeros((v.shape[0], 1), F32)
        left = jnp.concatenate([zero, v[:, : columns - 1]], axis=1)
        right = jnp.concatenate([v[:, 1:], zero], axis=1)
        parts = [x[16 * f : 16 * f + 16] for f in range(frames + 2) for x in (left, v, right)]
        taps[row] = jnp.concatenate(parts, axis=0).astype(BF16).T
    total = jnp.zeros((8, wall.shape[1]), F32)
    for t in range(frames):
        for r in range(rows - 2):
            patch = jnp.concatenate([taps[r + b, :, 48 * t : 48 * t + 144] for b in range(3)], axis=1)
            got = jnp.dot(patch, wall[...], preferred_element_type=F32).astype(BF16)
            first_ref[t, r] = got
            if 0 < r < rows - 3:
                total += jnp.sum(got.astype(F32).reshape(columns // 8, 8, -1), axis=0)
    count = frames * (rows - 4) * columns
    mean = jnp.sum(total, axis=0, keepdims=True) * (1.0 / count)
    square = jnp.zeros((8, wall.shape[1]), F32)
    for t in range(frames):
        for r in range(1, rows - 3):
            d = first_ref[t, r].astype(F32) - mean
            square += jnp.sum((d * d).reshape(columns // 8, 8, -1), axis=0)
    stat_ref[0:1, :] = mean
    stat_ref[1:2, :] = jnp.sum(square, axis=0, keepdims=True)


def scale_shift(means, squares, gain, count):
    channels = gain.shape[1]
    lane = lax.broadcasted_iota(jnp.int32, (channels, channels), 0) // GSIZE
    other = lax.broadcasted_iota(jnp.int32, (channels, channels), 1) // GSIZE
    same = (lane == other).astype(F32)

    def over_group(v):
        v = jnp.broadcast_to(v, (8, channels))
        return jnp.dot(v, same, precision=lax.Precision.HIGHEST, preferred_element_type=F32)[0:1]

    tiles = sum(m.shape[0] for m in means)
    mean = over_group(sum(jnp.sum(m, axis=0, keepdims=True) for m in means)) * (1.0 / (tiles * GSIZE))
    spread = jnp.zeros_like(mean)
    for m, q in zip(means, squares):
        spread += jnp.sum(q + float(count) * (m - mean) * (m - mean), axis=0, keepdims=True)
    variance = over_group(spread) * (1.0 / (count * tiles * GSIZE))
    scale = lax.rsqrt(variance + 1e-06) * gain
    return mean, scale


def put_row(taps, f, r, v):
    columns, channels = v.shape
    at = lax.broadcasted_iota(jnp.int32, v.shape, 0)
    left = jnp.where(at == 0, 0.0, pltpu.roll(v, 1, axis=0))
    right = jnp.where(at == columns - 1, 0.0, pltpu.roll(v, columns - 1, axis=0))
    taps[f, r, :, 0:channels] = left.astype(BF16)
    taps[f, r, :, channels : 2 * channels] = v.astype(BF16)
    taps[f, r, :, 2 * channels :] = right.astype(BF16)


def activate(v, mean, scale):
    y = (v - mean) * scale
    return (0.5 * y) * (1.0 + jnp.tanh(0.5 * y))


def row_sum(got, columns, inner):
    if not inner:
        return got[0] + got[1] + got[2]
    above, here, below = got
    head = here[:columns] + below[:columns]
    tail = here[-columns:] + above[-columns:]
    return jnp.concatenate([head, here[columns:-columns] + above[:-columns] + below[columns:], tail], axis=0)


def row_span(b, rows, inner):
    return (max(1, b), min(rows - 1, b + rows - 2)) if inner else (b, b + rows - 2)


def tap_product(taps, f, w_ref, lanes, inner=False):
    _, rows, columns, depth = taps.shape
    got = []
    for b in range(3):
        first, end = row_span(b, rows, inner)
        x = taps[f, first:end].reshape((end - first) * columns, depth)
        w = w_ref[3 * b : 3 * b + 3, :, lanes].reshape(depth, lanes.stop - lanes.start)
        got.append(jnp.dot(x, w, preferred_element_type=F32))
    return row_sum(got, columns, inner)


def lone_product(taps, f, w_ref, lanes, inner=False):
    _, rows, columns, depth = taps.shape
    depth //= 3
    outer, centre = [], []
    if not inner:
        x = [taps[f, b : b + rows - 2, :, depth : 2 * depth].reshape((rows - 2) * columns, depth) for b in range(3)]
        x = jnp.concatenate(x, axis=1)
        w = [jnp.concatenate([w_ref[3 * b + e, :, lanes] for b in range(3)], axis=0) for e in range(3)]
        outer = [jnp.dot(x, jnp.concatenate([w[0], w[2]], axis=1), preferred_element_type=F32), 0.0, 0.0]
        centre = [jnp.dot(x, w[1], preferred_element_type=F32), 0.0, 0.0]
    for b in range(0 if not inner else 3):
        first, end = row_span(b, rows, inner)
        x = taps[f, first:end, :, depth : 2 * depth].reshape((end - first) * columns, depth)
        pair = jnp.concatenate([w_ref[3 * b, :, lanes], w_ref[3 * b + 2, :, lanes]], axis=1)
        outer.append(jnp.dot(x, pair, preferred_element_type=F32))
        centre.append(jnp.dot(x, w_ref[3 * b + 1, :, lanes], preferred_element_type=F32))
    outer, centre = row_sum(outer, columns, inner), row_sum(centre, columns, inner)
    left, right = outer[:, 0:128], outer[:, 128:256]
    at = lax.broadcasted_iota(jnp.int32, left.shape, 0) % columns
    left = jnp.where(at == 0, 0.0, pltpu.roll(left, 1, axis=0))
    right = jnp.where(at == columns - 1, 0.0, pltpu.roll(right, left.shape[0] - 1, axis=0))
    return centre + left + right


def spread_rows(own, up, down, f, r, rows, channels):
    if r == 0:
        return up[f].astype(F32)
    if r == rows - 1:
        return down[f].astype(F32)
    lanes = slice((r - 1) * channels, r * channels)
    return jnp.concatenate([piece[f, :, lanes].astype(F32) for piece in own], axis=1)


def cached_body(p0, p1, p2, p3, early_ref, out_ref, taps):
    pieces = (p0, p1, p2, p3)
    rows = taps.shape[1]
    channels = p0.shape[2] // (rows - 2)
    for f in range(2):
        for r in range(rows):
            if 0 < r < rows - 1:
                v = spread_rows(pieces, None, None, f, r, rows, channels)
            else:
                at = (2 * f + (r > 0)) * channels
                v = jnp.concatenate([piece[2, :, at : at + channels].astype(F32) for piece in pieces], axis=1)
            put_row(taps, f, r, v)
    one = lone_product(taps, 0, early_ref, slice(128, 256))
    both = tap_product(taps, 1, early_ref, slice(0, 256))
    out_ref[0] = one + both[:, 0:128]
    out_ref[1] = both[:, 128:256]


def conv_current(taps, late_ref, early_ref, cached_ref, inner=False):
    both = tap_product(taps, 0, late_ref, slice(0, 256), inner)
    yield cached_ref[0] + both[:, 0:128]
    middle = cached_ref[1] + both[:, 128:256]
    last = lone_product(taps, 0, early_ref, slice(128, 256), inner)
    both = tap_product(taps, 1, late_ref, slice(0, 256), inner)
    yield middle + both[:, 0:128]
    last = last + both[:, 128:256]
    yield last + lone_product(taps, 2, late_ref, slice(0, 128), inner)


def gain_of(refs, n, channels):
    at = refs[0].shape[0] - 16
    n += 27 % GROUP
    lanes = slice(n * channels, (n + 1) * channels)
    terms = [ref[at : at + 16, lanes].astype(F32) for ref in refs]
    return jnp.concatenate([(t[0:1] + t[1:2]) + t[2:3] for t in terms], axis=1)


def inside():
    t = lax.axis_index("tile")
    return (t > 0).astype(F32), (t < lax.axis_size("tile") - 1).astype(F32)


def middle_body(n_stats, count, *refs):
    stats = refs[:n_stats]
    gains = refs[n_stats : n_stats + 4]
    first_ref, cached_ref, late_ref, early_ref, out_ref, stat_ref, taps, kept = refs[n_stats + 4 :]
    edges = inside()
    means = [s[:, 0, :] for s in stats]
    squares = [s[:, 1, :] for s in stats]
    mean, scale = scale_shift(means, squares, gain_of(gains, 0, first_ref.shape[3] // 4), count)
    frames, rows, columns, _ = taps.shape
    for f in range(frames):
        for r in range(rows):
            v = activate(first_ref[f, r].astype(F32), mean, scale)
            if r == 0:
                v = v * edges[0]
            if r == rows - 1:
                v = v * edges[1]
            put_row(taps, f, r, v)
    channels = out_ref.shape[2] // (rows - 2)
    total = jnp.zeros((1, 128), F32)
    for f, got in enumerate(conv_current(taps, late_ref, early_ref, cached_ref)):
        kept[f] = got
        total += jnp.sum(got, axis=0, keepdims=True)
        parts = [got[h * columns : (h + 1) * columns, 0:channels] for h in range(rows - 2)]
        out_ref[f] = jnp.concatenate(parts, axis=1).astype(BF16)
    local = total * (1.0 / (frames * (rows - 2) * columns))
    square = jnp.zeros((1, 128), F32)
    for f in range(frames):
        d = kept[f] - local
        square += jnp.sum(d * d, axis=0, keepdims=True)
    stat_ref[0:1, :] = local
    stat_ref[1:2, :] = square


def last_body(n_stats, count, *refs):
    stats = refs[:n_stats]
    gains, (p0, p1, p2, *p3) = refs[n_stats : n_stats + 4], refs[n_stats + 4 : n_stats + 9]
    cached_ref, late_ref, early_ref, out_ref, scale_ref, taps = refs[n_stats + 9 :]
    frames, rows, _, _ = taps.shape
    channels = p0.shape[2] // (rows - 2)

    def wide(s, n):
        return jnp.concatenate([s[:, slot, n, 0:channels] for slot in range(4)], axis=1)

    means = [wide(s, 0) for s in stats]
    squares = [wide(s, 1) for s in stats]
    mean, scale = scale_shift(means, squares, gain_of(gains, 1, channels), count)
    scale_ref[0:1, :] = mean
    scale_ref[1:2, :] = scale
    for f in range(frames):
        for r in range(1, rows - 1):
            at = slice((r - 1) * channels, r * channels)
            far = jnp.concatenate([piece[f, :, at].astype(F32) for piece in p3], axis=0)
            v = jnp.concatenate([piece[f, :, at].astype(F32) for piece in (p0, p1, p2)] + [far], axis=1)
            put_row(taps, f, r, activate(v, mean, scale))
    for f, got in enumerate(conv_current(taps, late_ref, early_ref, cached_ref, True)):
        out_ref[f] = got


def edge_body(part_ref, scale_ref, up, down, first_ref, late_ref, early_ref, out_hbm, taps, out_ref, sems):
    frames, _, columns, depth = taps.shape
    rows = first_ref.shape[1]
    channels = out_ref.shape[3]
    mean, scale = scale_ref[0:1, :], scale_ref[1:2, :]
    added = []
    for side, (ref, kept, b) in enumerate(zip((up, down), inside(), (0, 2))):
        for f in range(frames):
            put_row(taps, f, side, activate(ref[f].astype(F32), mean, scale) * kept)
        taken = slice(3 * b, 3 * b + 3)
        x = jnp.concatenate([taps[f, side] for f in range(frames)], axis=0)
        both = jnp.dot(x, late_ref[taken].reshape(depth, 256), preferred_element_type=F32)
        late = jnp.dot(taps[0, side], early_ref[taken, :, 128:256].reshape(depth, 128), preferred_element_type=F32)
        now, then = both[:, 0:128], both[:, 128:256]
        added.append(
            [
                now[0:columns],
                now[columns : 2 * columns] + then[0:columns],
                now[2 * columns :] + then[columns : 2 * columns] + late,
            ]
        )
    for f in range(frames):
        for h in range(rows - 2):
            here = part_ref[f, h * columns : (h + 1) * columns]
            if h == 0:
                here = here + added[0][f]
            if h == rows - 3:
                here = here + added[1][f]
            here = here[:, 0:channels] + first_ref[f, h + 1][:, 0:channels].astype(F32)
            out_ref[f, h] = here.astype(BF16)
        pltpu.make_async_copy(out_ref.at[f], out_hbm.at[f], sems.at[f]).start()
    for f in range(frames):
        pltpu.make_async_copy(out_ref.at[f], out_hbm.at[f], sems.at[f]).wait()


def edges_of(pieces, channels):
    top = jnp.concatenate([p[:, :, :channels] for p in pieces], axis=2)
    bottom = jnp.concatenate([p[:, :, -channels:] for p in pieces], axis=2)
    return to_next(bottom), to_previous(top)


def shaped(shape, dtype):
    return jax.ShapeDtypeStruct(tuple(shape), dtype)


def window(
    latent,
    row_map,
    latent_cache,
    cache_one,
    cache_two,
    conv_in_w,
    weight_one,
    weight_two,
    gain_one,
    gain_two,
):
    frames, _, lc, columns = latent.shape
    tile_rows = latent_cache.shape[1]
    tiles, sources = lax.axis_size("tile"), lax.axis_size("src")
    channels = conv_in_w.shape[4]
    wide = channels * sources
    others = range(1, sources)

    taps = 27 * lc
    height = lc + -(-27 // GROUP) * lc
    message = call(
        message_body,
        shaped((height, frames * columns), BF16),
        scratch=[
            pltpu.VMEM(latent.shape, BF16),
            pltpu.VMEM((1, channels), F32),
            pltpu.VMEM((1, channels), F32),
            pltpu.VMEM((taps, channels), BF16),
            pltpu.SemaphoreType.DMA((4,)),
        ],
        specs=[HBM] * 4,
    )(*stay(latent, gain_one[None], gain_two[None], conv_in_w.reshape(taps, channels)))
    got = xor_stage(message, "src", others)
    near = call(near_body, shaped((sources, lc, frames * columns), BF16), n_in=sources)(*got)
    for masks in far_masks(tiles):
        near = jnp.concatenate(xor_stage(near, "tile", masks), axis=0)
    far = xor_send(near, "tile", 1)

    caches = (cache_one.transpose(0, 1, 3, 2), cache_two.transpose(0, 1, 3, 2), latent_cache)
    strip = shaped((columns + 2 * lc, tile_rows * channels), BF16)
    rimmed = shaped((3, columns, tile_rows * channels), BF16)
    own_one, own_two, span, low, high = call(
        pack_body,
        (rimmed, rimmed, shaped((tile_rows, lc, 2 * columns), BF16), strip, strip),
        scratch=[pltpu.VMEM(x.shape, BF16) for x in caches] + [pltpu.SemaphoreType.DMA((3,))],
        specs=[HBM] * 3,
    )(*stay(*caches))
    before = to_next(high)
    after = to_previous(low)
    rim_one, rim_two = call(
        rim_body,
        (rimmed, rimmed),
        scratch=[pltpu.VMEM((2, columns, tile_rows * channels), BF16), pltpu.SemaphoreType.DMA((2,))],
        specs=[HBM, HBM, VMEM, VMEM],
        out_specs=(HBM, HBM),
        alias={0: 0, 1: 1},
    )(own_one, own_two, before, after)
    pieces_one = xor_stage(rim_one, "src", others)
    pieces_two = xor_stage(rim_two, "src", others)

    def turn(w):
        shape = shaped((9, wide, 256), BF16)
        return call(weights_body, (shape, shape), scratch=[pltpu.VMEM((3, wide, 128), BF16)], n_in=1)(w)

    late_one, early_one = turn(weight_one)
    late_two, early_two = turn(weight_two)

    rows = tile_rows + 2
    spots = tile_rows * columns
    flops = 2 * 27 * wide * channels * spots

    def cached(pieces, early):
        return call(
            cached_body,
            shaped((2, spots, 128), F32),
            flops=flops,
            scratch=[pltpu.VMEM((2, rows, columns, 3 * wide), BF16)],
            n_in=5,
        )(*pieces, early)

    cached_one = cached(pieces_one, early_one)
    cached_two = cached(pieces_two, early_two)

    first, stat = call(
        first_body,
        (shaped((frames, rows, columns, wide), BF16), shaped((2, wide), F32)),
        flops=flops // 4,
        scratch=[
            pltpu.VMEM((rows + 2, columns, (frames + 2) * 3 * lc), BF16),
            pltpu.VMEM((27 * lc, wide), BF16),
            pltpu.SMEM((rows + 2,), jnp.int32),
        ],
        specs=[SMEM] + [VMEM] * 9,
    )(row_map, near, far, before, span, after, *got)

    def over_tiles(x, stages):
        x = jnp.stack(xor_stage(x, "tile", [1]))
        for masks in stages[:-1]:
            x = jnp.concatenate(xor_stage(x, "tile", masks), axis=0)
        return xor_stage(x, "tile", stages[-1])

    doubling = [[1 << n] for n in range(1, tiles.bit_length() - 1)]
    count = frames * spots
    stats = over_tiles(stat, doubling)
    middle, stat_two = call(
        functools.partial(middle_body, len(stats), count),
        (shaped((frames, columns, tile_rows * channels), BF16), shaped((2, 128), F32)),
        flops=flops * 2,
        scratch=[
            pltpu.VMEM((frames, rows, columns, 3 * wide), BF16),
            pltpu.VMEM((frames, spots, 128), F32),
        ],
        n_in=len(stats) + 8,
    )(*stats, *got, first, cached_one, late_one, early_one)

    mids = xor_stage(middle, "src", [1, 2])
    cut = columns // 2
    mids += [xor_send(mids[1][:, :cut], "src", 2), xor_send(mids[2][:, cut:], "src", 1)]
    stats = over_tiles(jnp.stack(xor_stage(stat_two, "src", others)), far_masks(tiles))
    above, below = edges_of(mids[:3] + [jnp.concatenate(mids[3:], axis=1)], channels)
    part, scales = call(
        functools.partial(last_body, len(stats), count),
        (shaped((frames, spots, 128), F32), shaped((2, wide), F32)),
        flops=flops * 2,
        scratch=[pltpu.VMEM((frames, rows, columns, 3 * wide), BF16)],
        n_in=len(stats) + 12,
    )(*stats, *got, *mids, cached_two, late_two, early_two)
    decoded = call(
        edge_body,
        shaped((frames, tile_rows, columns, channels), BF16),
        flops=flops // 2,
        scratch=[
            pltpu.VMEM((frames, 2, columns, 3 * wide), BF16),
            pltpu.VMEM((frames, tile_rows, columns, channels), BF16),
            pltpu.SemaphoreType.DMA((frames,)),
        ],
        n_in=7,
        out_specs=HBM,
    )(part, scales, above, below, first, late_two, early_two)
    return decoded.transpose(0, 1, 3, 2)


def solution(mesh):
    placed = (
        P(None, ("src", "tile"), None, None),
        P(),
        P(None, "tile", None, None),
        P(None, "tile", "src", None),
        P(None, "tile", "src", None),
        P(None, None, None, None, "src"),
        P(None, None, None, "src", None),
        P(None, None, None, "src", None),
        P("src"),
        P("src"),
    )
    return jax.shard_map(
        window,
        mesh=mesh,
        in_specs=placed,
        out_specs=P(None, "tile", "src", None),
        check_vma=False,
    )
```

```python
import functools

import jax
import jax.numpy as jnp
from jax import lax
from jax.experimental import pallas as pl
from jax.experimental.pallas import tpu as pltpu
from jax.sharding import PartitionSpec as P


GSIZE = 12
F32 = jnp.float32
BF16 = jnp.bfloat16
VMEM_LIMIT = 24 << 20
VMEM = pl.BlockSpec(memory_space=pltpu.VMEM)
SMEM = pl.BlockSpec(memory_space=pltpu.SMEM)
HBM = pl.BlockSpec(memory_space=pl.ANY)


def call(body, outs, flops=0, scratch=(), specs=None, n_in=0, out_specs=None, limit=VMEM_LIMIT, alias=None):
    return pl.pallas_call(
        body,
        out_shape=outs,
        in_specs=specs if specs is not None else [VMEM] * n_in,
        out_specs=out_specs if out_specs is not None else jax.tree.map(lambda _: VMEM, outs),
        scratch_shapes=list(scratch),
        input_output_aliases=alias or {},
        cost_estimate=pl.CostEstimate(flops=flops, bytes_accessed=1 << 20, transcendentals=0),
        compiler_params=pltpu.CompilerParams(vmem_limit_bytes=limit),
    )


def xor_send(x, axis, mask):
    return lax.ppermute(x, axis, [(i, i ^ mask) for i in range(lax.axis_size(axis))])


def xor_stage(x, axis, masks):
    return [x] + [xor_send(x, axis, m) for m in masks]


def far_masks(size):
    low, stages = 2, []
    while low < size:
        if low * 2 < size:
            stages.append([low, 2 * low, 3 * low])
            low *= 4
        else:
            stages.append([low])
            low *= 2
    return stages


def stay(*arrays):
    return [pltpu.with_memory_space_constraint(x, pltpu.HBM) for x in arrays]


def to_next(x):
    return lax.ppermute(x, "tile", [(i, i + 1) for i in range(lax.axis_size("tile") - 1)])


def to_previous(x):
    return lax.ppermute(x, "tile", [(i + 1, i) for i in range(lax.axis_size("tile") - 1)])


def fetch(sources, targets, sems):
    copies = [pltpu.make_async_copy(src, dst, sems.at[n]) for n, (src, dst) in enumerate(zip(sources, targets))]
    for copy in copies:
        copy.start()
    for copy in copies:
        copy.wait()


GROUP = 5


def message_body(*refs):
    out_ref, latent_ref, gain_a, gain_b, w_ref, sems = refs[4:]
    fetch(refs[:4], (latent_ref, gain_a, gain_b, w_ref), sems)
    lc, channels = latent_ref.shape[2], gain_a.shape[1]

    def joined(parts):
        return jnp.concatenate([part.astype(F32) for part in parts], axis=1).astype(BF16)

    out_ref[0:lc, :] = joined([latent_ref[f, 0] for f in range(latent_ref.shape[0])])
    taps = w_ref.shape[0] // lc
    for n in range(0, taps, GROUP):
        held = [w_ref[k * lc : (k + 1) * lc] for k in range(n, min(n + GROUP, taps))]
        at = lc + n // GROUP * lc
        out_ref[at : at + lc, 0 : len(held) * channels] = joined(held)
    gains = jnp.concatenate([gain_a[...], gain_b[...]], axis=1)
    at = out_ref.shape[0] - 16
    terms = []
    for _ in range(3):
        terms.append(gains.astype(BF16).astype(F32))
        gains = gains - terms[-1]
    rows = jnp.concatenate(terms + [jnp.zeros((13, gains.shape[1]), F32)], axis=0)
    lane = taps % GROUP * channels
    out_ref[at:, lane : lane + gains.shape[1]] = rows.astype(BF16)


def near_body(*refs):
    out_ref = refs[-1]
    for n, ref in enumerate(refs[:-1]):
        out_ref[n] = ref[0 : out_ref.shape[1], :]


def pack_body(*refs):
    own_one, own_two, span_out, low_ref, high_ref, *here, sems = refs[3:]
    fetch(refs[:3], here, sems)
    one_ref, two_ref, span_ref = here
    frames, rows = one_ref.shape[0], one_ref.shape[1]
    columns, lc = one_ref.shape[2], span_ref.shape[2]

    def joined(parts):
        return jnp.concatenate([part.astype(F32) for part in parts], axis=1).astype(BF16)

    for ref, out in ((one_ref, own_one), (two_ref, own_two)):
        for f in range(frames):
            out[f] = joined([ref[f, h] for h in range(rows)])
    every = [ref.at[f] for ref in (one_ref, two_ref) for f in range(frames)]
    low_ref[0:columns, :] = joined([ref[0] for ref in every])
    high_ref[0:columns, :] = joined([ref[rows - 1] for ref in every])
    width = span_ref.shape[3] * frames
    for ref in (low_ref, high_ref):
        ref[columns:, :] = jnp.zeros_like(ref[columns:, :])
    for row in range(rows):
        both = joined([span_ref[f, row] for f in range(frames)])
        span_out[row] = both
        if row < 2:
            low_ref[columns + row * lc : columns + (row + 1) * lc, 0:width] = both
        if row >= rows - 2:
            at = columns + (row - rows + 2) * lc
            high_ref[at : at + lc, 0:width] = both


def rim_body(one_in, two_in, before, after, one_out, two_out, held, sems):
    columns = held.shape[1]
    channels = held.shape[2] // 4
    copies = []
    for n, out in enumerate((one_out, two_out)):
        parts = []
        for f in range(2):
            lanes = slice((2 * n + f) * channels, (2 * n + f + 1) * channels)
            parts += [side[0:columns, lanes].astype(F32) for side in (before, after)]
        held[n] = jnp.concatenate(parts, axis=1).astype(BF16)
        copies.append(pltpu.make_async_copy(held.at[n], out.at[2], sems.at[n]))
        copies[-1].start()
    for copy in copies:
        copy.wait()


def weights_body(w_ref, late_ref, early_ref, turned):
    outs, ins = w_ref.shape[3], w_ref.shape[4]
    mine = lax.axis_index("src")
    turned[...] = jnp.zeros_like(turned)

    def tap(n, _):
        b, e = n // 3, n % 3
        for a in range(3):
            turned[a, :, 0:outs] = w_ref[a, b, e].T
        for slot in range(ins // outs):
            start = pl.multiple_of(jnp.bitwise_xor(mine, slot) * outs, 16)
            here = pl.ds(slot * outs, outs)
            early, middle, late = [turned[a, pl.ds(start, outs), :] for a in range(3)]
            late_ref[n, here, 0:128] = late
            late_ref[n, here, 128:256] = middle
            early_ref[n, here, 0:128] = middle
            early_ref[n, here, 128:256] = early
        return 0

    lax.fori_loop(0, 9, tap, 0)


def first_body(map_ref, near_ref, far_ref, before, own, after, m0, m1, m2, m3, first_ref, stat_ref, taps, wall, tab_ref):
    half = near_ref.shape[0]
    rows = own.shape[0] + 4
    columns = own.shape[2] // 2
    frames = near_ref.shape[2] // columns
    s, t, tiles = lax.axis_index("src"), lax.axis_index("tile"), lax.axis_size("tile")
    top = t * (rows - 4) - 2
    for row in range(rows):
        tab_ref[row] = -1
    for i in range(map_ref.shape[0]):
        at = map_ref[i] - top
        to_t, to_s = jnp.bitwise_xor(i % tiles, t), jnp.bitwise_xor(i // tiles, s)
        place = to_t % 2 * half + to_t // 2 * 4 + to_s

        @pl.when(jnp.logical_and(at >= 0, at < rows))
        def _():
            tab_ref[jnp.clip(at, 0, rows - 1)] = place

    wide = wall.shape[1]
    for n in range(wall.shape[0] // 16):
        at, lanes = 16 + n // GROUP * 16, slice(n % GROUP * wide // 4, (n % GROUP + 1) * wide // 4)
        parts = [m[at : at + 16, lanes].astype(F32) for m in (m0, m1, m2, m3)]
        a, b, e = n // 9, n // 3 % 3, n % 3
        put = 16 * (9 * b + 3 * a + e)
        wall[put : put + 16, :] = jnp.concatenate(parts, axis=1).astype(BF16)
    for row in range(rows):
        place = tab_ref[row]
        kept = (place >= 0).astype(F32)
        inner = jnp.maximum(jnp.where(place >= half, place - half, place), 0)
        new = jnp.where(place >= half, far_ref[inner].astype(F32), near_ref[inner].astype(F32)) * kept
        if 2 <= row < rows - 2:
            old = own[row - 2].astype(F32)
        else:
            at = columns + 16 * (row if row < 2 else row - rows + 2)
            old = (before if row < 2 else after)[at : at + 16, 0 : 2 * columns].astype(F32)
        line = [old[:, f * columns : (f + 1) * columns] for f in range(2)]
        line += [new[:, f * columns : (f + 1) * columns] for f in range(frames)]
        v = jnp.concatenate(line, axis=0)
        zero = jnp.zeros((v.shape[0], 1), F32)
        left = jnp.concatenate([zero, v[:, : columns - 1]], axis=1)
        right = jnp.concatenate([v[:, 1:], zero], axis=1)
        parts = [x[16 * f : 16 * f + 16] for f in range(frames + 2) for x in (left, v, right)]
        taps[row] = jnp.concatenate(parts, axis=0).astype(BF16).T
    total = jnp.zeros((8, wall.shape[1]), F32)
    for t in range(frames):
        for r in range(rows - 2):
            patch = jnp.concatenate([taps[r + b, :, 48 * t : 48 * t + 144] for b in range(3)], axis=1)
            got = jnp.dot(patch, wall[...], preferred_element_type=F32).astype(BF16)
            first_ref[t, r] = got
            if 0 < r < rows - 3:
                total += jnp.sum(got.astype(F32).reshape(columns // 8, 8, -1), axis=0)
    count = frames * (rows - 4) * columns
    mean = jnp.sum(total, axis=0, keepdims=True) * (1.0 / count)
    square = jnp.zeros((8, wall.shape[1]), F32)
    for t in range(frames):
        for r in range(1, rows - 3):
            d = first_ref[t, r].astype(F32) - mean
            square += jnp.sum((d * d).reshape(columns // 8, 8, -1), axis=0)
    stat_ref[0:1, :] = mean
    stat_ref[1:2, :] = jnp.sum(square, axis=0, keepdims=True)


def scale_shift(means, squares, gain, count):
    channels = gain.shape[1]
    lane = lax.broadcasted_iota(jnp.int32, (channels, channels), 0) // GSIZE
    other = lax.broadcasted_iota(jnp.int32, (channels, channels), 1) // GSIZE
    same = (lane == other).astype(F32)

    def over_group(v):
        v = jnp.broadcast_to(v, (8, channels))
        return jnp.dot(v, same, precision=lax.Precision.HIGHEST, preferred_element_type=F32)[0:1]

    tiles = sum(m.shape[0] for m in means)
    mean = over_group(sum(jnp.sum(m, axis=0, keepdims=True) for m in means)) * (1.0 / (tiles * GSIZE))
    spread = jnp.zeros_like(mean)
    for m, q in zip(means, squares):
        spread += jnp.sum(q + float(count) * (m - mean) * (m - mean), axis=0, keepdims=True)
    variance = over_group(spread) * (1.0 / (count * tiles * GSIZE))
    scale = lax.rsqrt(variance + 1e-06) * gain
    return mean, scale


def put_row(taps, f, r, v):
    columns, channels = v.shape
    edge = jnp.zeros((1, channels), F32)
    left = jnp.concatenate([edge, v[: columns - 1]], axis=0)
    right = jnp.concatenate([v[1:], edge], axis=0)
    taps[f, r, :, 0:channels] = left.astype(BF16)
    taps[f, r, :, channels : 2 * channels] = v.astype(BF16)
    taps[f, r, :, 2 * channels :] = right.astype(BF16)


def activate(v, mean, scale):
    y = (v - mean) * scale
    return (0.5 * y) * (1.0 + jnp.tanh(0.5 * y))


def row_sum(got, columns, inner):
    if not inner:
        return got[0] + got[1] + got[2]
    above, here, below = got
    head = here[:columns] + below[:columns]
    tail = here[-columns:] + above[-columns:]
    return jnp.concatenate([head, here[columns:-columns] + above[:-columns] + below[columns:], tail], axis=0)


def row_span(b, rows, inner):
    return (max(1, b), min(rows - 1, b + rows - 2)) if inner else (b, b + rows - 2)


def tap_product(taps, f, w_ref, lanes, inner=False):
    _, rows, columns, depth = taps.shape
    got = []
    for b in range(3):
        first, end = row_span(b, rows, inner)
        x = taps[f, first:end].reshape((end - first) * columns, depth)
        w = w_ref[3 * b : 3 * b + 3, :, lanes].reshape(depth, lanes.stop - lanes.start)
        got.append(jnp.dot(x, w, preferred_element_type=F32))
    return row_sum(got, columns, inner)


def lone_product(taps, f, w_ref, lanes, inner=False):
    _, rows, columns, depth = taps.shape
    depth //= 3
    outer, centre = [], []
    if not inner:
        x = [taps[f, b : b + rows - 2, :, depth : 2 * depth].reshape((rows - 2) * columns, depth) for b in range(3)]
        x = jnp.concatenate(x, axis=1)
        w = [jnp.concatenate([w_ref[3 * b + e, :, lanes] for b in range(3)], axis=0) for e in range(3)]
        outer = [jnp.dot(x, jnp.concatenate([w[0], w[2]], axis=1), preferred_element_type=F32), 0.0, 0.0]
        centre = [jnp.dot(x, w[1], preferred_element_type=F32), 0.0, 0.0]
    for b in range(0 if not inner else 3):
        first, end = row_span(b, rows, inner)
        x = taps[f, first:end, :, depth : 2 * depth].reshape((end - first) * columns, depth)
        pair = jnp.concatenate([w_ref[3 * b, :, lanes], w_ref[3 * b + 2, :, lanes]], axis=1)
        outer.append(jnp.dot(x, pair, preferred_element_type=F32))
        centre.append(jnp.dot(x, w_ref[3 * b + 1, :, lanes], preferred_element_type=F32))
    outer, centre = row_sum(outer, columns, inner), row_sum(centre, columns, inner)
    left, right = outer[:, 0:128], outer[:, 128:256]
    at = lax.broadcasted_iota(jnp.int32, left.shape, 0) % columns
    left = jnp.where(at == 0, 0.0, pltpu.roll(left, 1, axis=0))
    right = jnp.where(at == columns - 1, 0.0, pltpu.roll(right, left.shape[0] - 1, axis=0))
    return centre + left + right


def spread_rows(own, up, down, f, r, rows, channels):
    if r == 0:
        return up[f].astype(F32)
    if r == rows - 1:
        return down[f].astype(F32)
    lanes = slice((r - 1) * channels, r * channels)
    return jnp.concatenate([piece[f, :, lanes].astype(F32) for piece in own], axis=1)


def cached_body(p0, p1, p2, p3, early_ref, out_ref, taps):
    pieces = (p0, p1, p2, p3)
    rows = taps.shape[1]
    channels = p0.shape[2] // (rows - 2)
    for f in range(2):
        for r in range(rows):
            if 0 < r < rows - 1:
                v = spread_rows(pieces, None, None, f, r, rows, channels)
            else:
                at = (2 * f + (r > 0)) * channels
                v = jnp.concatenate([piece[2, :, at : at + channels].astype(F32) for piece in pieces], axis=1)
            put_row(taps, f, r, v)
    one = lone_product(taps, 0, early_ref, slice(128, 256))
    both = tap_product(taps, 1, early_ref, slice(0, 256))
    out_ref[0] = one + both[:, 0:128]
    out_ref[1] = both[:, 128:256]


def conv_current(taps, late_ref, early_ref, cached_ref, inner=False):
    both = tap_product(taps, 0, late_ref, slice(0, 256), inner)
    yield cached_ref[0] + both[:, 0:128]
    middle = cached_ref[1] + both[:, 128:256]
    last = lone_product(taps, 0, early_ref, slice(128, 256), inner)
    both = tap_product(taps, 1, late_ref, slice(0, 256), inner)
    yield middle + both[:, 0:128]
    last = last + both[:, 128:256]
    yield last + lone_product(taps, 2, late_ref, slice(0, 128), inner)


def gain_of(refs, n, channels):
    at = refs[0].shape[0] - 16
    n += 27 % GROUP
    lanes = slice(n * channels, (n + 1) * channels)
    terms = [ref[at : at + 16, lanes].astype(F32) for ref in refs]
    return jnp.concatenate([(t[0:1] + t[1:2]) + t[2:3] for t in terms], axis=1)


def inside():
    t = lax.axis_index("tile")
    return (t > 0).astype(F32), (t < lax.axis_size("tile") - 1).astype(F32)


def middle_body(n_stats, count, *refs):
    stats = refs[:n_stats]
    gains = refs[n_stats : n_stats + 4]
    first_ref, cached_ref, late_ref, early_ref, out_ref, stat_ref, taps, kept = refs[n_stats + 4 :]
    edges = inside()
    means = [s[:, 0, :] for s in stats]
    squares = [s[:, 1, :] for s in stats]
    mean, scale = scale_shift(means, squares, gain_of(gains, 0, first_ref.shape[3] // 4), count)
    frames, rows, columns, _ = taps.shape
    for f in range(frames):
        for r in range(rows):
            v = activate(first_ref[f, r].astype(F32), mean, scale)
            if r == 0:
                v = v * edges[0]
            if r == rows - 1:
                v = v * edges[1]
            put_row(taps, f, r, v)
    channels = out_ref.shape[2] // (rows - 2)
    total = jnp.zeros((1, 128), F32)
    for f, got in enumerate(conv_current(taps, late_ref, early_ref, cached_ref)):
        kept[f] = got
        total += jnp.sum(got, axis=0, keepdims=True)
        parts = [got[h * columns : (h + 1) * columns, 0:channels] for h in range(rows - 2)]
        out_ref[f] = jnp.concatenate(parts, axis=1).astype(BF16)
    local = total * (1.0 / (frames * (rows - 2) * columns))
    square = jnp.zeros((1, 128), F32)
    for f in range(frames):
        d = kept[f] - local
        square += jnp.sum(d * d, axis=0, keepdims=True)
    stat_ref[0:1, :] = local
    stat_ref[1:2, :] = square


def last_body(n_stats, count, *refs):
    stats = refs[:n_stats]
    gains, (p0, p1, p2, *p3) = refs[n_stats : n_stats + 4], refs[n_stats + 4 : n_stats + 9]
    cached_ref, late_ref, early_ref, out_ref, scale_ref, taps = refs[n_stats + 9 :]
    frames, rows, _, _ = taps.shape
    channels = p0.shape[2] // (rows - 2)

    def wide(s, n):
        return jnp.concatenate([s[:, slot, n, 0:channels] for slot in range(4)], axis=1)

    means = [wide(s, 0) for s in stats]
    squares = [wide(s, 1) for s in stats]
    mean, scale = scale_shift(means, squares, gain_of(gains, 1, channels), count)
    scale_ref[0:1, :] = mean
    scale_ref[1:2, :] = scale
    for f in range(frames):
        for r in range(1, rows - 1):
            at = slice((r - 1) * channels, r * channels)
            far = jnp.concatenate([piece[f, :, at].astype(F32) for piece in p3], axis=0)
            v = jnp.concatenate([piece[f, :, at].astype(F32) for piece in (p0, p1, p2)] + [far], axis=1)
            put_row(taps, f, r, activate(v, mean, scale))
    for f, got in enumerate(conv_current(taps, late_ref, early_ref, cached_ref, True)):
        out_ref[f] = got


def edge_body(part_ref, scale_ref, up, down, first_ref, late_ref, early_ref, out_hbm, taps, out_ref, sems):
    frames, _, columns, depth = taps.shape
    rows = first_ref.shape[1]
    channels = out_ref.shape[3]
    mean, scale = scale_ref[0:1, :], scale_ref[1:2, :]
    added = []
    for side, (ref, kept, b) in enumerate(zip((up, down), inside(), (0, 2))):
        for f in range(frames):
            put_row(taps, f, side, activate(ref[f].astype(F32), mean, scale) * kept)
        taken = slice(3 * b, 3 * b + 3)
        x = jnp.concatenate([taps[f, side] for f in range(frames)], axis=0)
        both = jnp.dot(x, late_ref[taken].reshape(depth, 256), preferred_element_type=F32)
        late = jnp.dot(taps[0, side], early_ref[taken, :, 128:256].reshape(depth, 128), preferred_element_type=F32)
        now, then = both[:, 0:128], both[:, 128:256]
        added.append(
            [
                now[0:columns],
                now[columns : 2 * columns] + then[0:columns],
                now[2 * columns :] + then[columns : 2 * columns] + late,
            ]
        )
    for f in range(frames):
        for h in range(rows - 2):
            here = part_ref[f, h * columns : (h + 1) * columns]
            if h == 0:
                here = here + added[0][f]
            if h == rows - 3:
                here = here + added[1][f]
            here = here[:, 0:channels] + first_ref[f, h + 1][:, 0:channels].astype(F32)
            out_ref[f, h] = here.astype(BF16)
        pltpu.make_async_copy(out_ref.at[f], out_hbm.at[f], sems.at[f]).start()
    for f in range(frames):
        pltpu.make_async_copy(out_ref.at[f], out_hbm.at[f], sems.at[f]).wait()


def edges_of(pieces, channels):
    top = jnp.concatenate([p[:, :, :channels] for p in pieces], axis=2)
    bottom = jnp.concatenate([p[:, :, -channels:] for p in pieces], axis=2)
    return to_next(bottom), to_previous(top)


def shaped(shape, dtype):
    return jax.ShapeDtypeStruct(tuple(shape), dtype)


def window(
    latent,
    row_map,
    latent_cache,
    cache_one,
    cache_two,
    conv_in_w,
    weight_one,
    weight_two,
    gain_one,
    gain_two,
):
    frames, _, lc, columns = latent.shape
    tile_rows = latent_cache.shape[1]
    tiles, sources = lax.axis_size("tile"), lax.axis_size("src")
    channels = conv_in_w.shape[4]
    wide = channels * sources
    others = range(1, sources)

    taps = 27 * lc
    height = lc + -(-27 // GROUP) * lc
    message = call(
        message_body,
        shaped((height, frames * columns), BF16),
        scratch=[
            pltpu.VMEM(latent.shape, BF16),
            pltpu.VMEM((1, channels), F32),
            pltpu.VMEM((1, channels), F32),
            pltpu.VMEM((taps, channels), BF16),
            pltpu.SemaphoreType.DMA((4,)),
        ],
        specs=[HBM] * 4,
    )(*stay(latent, gain_one[None], gain_two[None], conv_in_w.reshape(taps, channels)))
    got = xor_stage(message, "src", others)
    near = call(near_body, shaped((sources, lc, frames * columns), BF16), n_in=sources)(*got)
    for masks in far_masks(tiles):
        near = jnp.concatenate(xor_stage(near, "tile", masks), axis=0)
    far = xor_send(near, "tile", 1)

    caches = (cache_one.transpose(0, 1, 3, 2), cache_two.transpose(0, 1, 3, 2), latent_cache)
    strip = shaped((columns + 2 * lc, tile_rows * channels), BF16)
    rimmed = shaped((3, columns, tile_rows * channels), BF16)
    own_one, own_two, span, low, high = call(
        pack_body,
        (rimmed, rimmed, shaped((tile_rows, lc, 2 * columns), BF16), strip, strip),
        scratch=[pltpu.VMEM(x.shape, BF16) for x in caches] + [pltpu.SemaphoreType.DMA((3,))],
        specs=[HBM] * 3,
    )(*stay(*caches))
    before = to_next(high)
    after = to_previous(low)
    rim_one, rim_two = call(
        rim_body,
        (rimmed, rimmed),
        scratch=[pltpu.VMEM((2, columns, tile_rows * channels), BF16), pltpu.SemaphoreType.DMA((2,))],
        specs=[HBM, HBM, VMEM, VMEM],
        out_specs=(HBM, HBM),
        alias={0: 0, 1: 1},
    )(own_one, own_two, before, after)
    pieces_one = xor_stage(rim_one, "src", others)
    pieces_two = xor_stage(rim_two, "src", others)

    def turn(w):
        shape = shaped((9, wide, 256), BF16)
        return call(weights_body, (shape, shape), scratch=[pltpu.VMEM((3, wide, 128), BF16)], n_in=1)(w)

    late_one, early_one = turn(weight_one)
    late_two, early_two = turn(weight_two)

    rows = tile_rows + 2
    spots = tile_rows * columns
    flops = 2 * 27 * wide * channels * spots

    def cached(pieces, early):
        return call(
            cached_body,
            shaped((2, spots, 128), F32),
            flops=flops,
            scratch=[pltpu.VMEM((2, rows, columns, 3 * wide), BF16)],
            n_in=5,
        )(*pieces, early)

    cached_one = cached(pieces_one, early_one)
    cached_two = cached(pieces_two, early_two)

    first, stat = call(
        first_body,
        (shaped((frames, rows, columns, wide), BF16), shaped((2, wide), F32)),
        flops=flops // 4,
        scratch=[
            pltpu.VMEM((rows + 2, columns, (frames + 2) * 3 * lc), BF16),
            pltpu.VMEM((27 * lc, wide), BF16),
            pltpu.SMEM((rows + 2,), jnp.int32),
        ],
        specs=[SMEM] + [VMEM] * 9,
    )(row_map, near, far, before, span, after, *got)

    def over_tiles(x, stages):
        x = jnp.stack(xor_stage(x, "tile", [1]))
        for masks in stages[:-1]:
            x = jnp.concatenate(xor_stage(x, "tile", masks), axis=0)
        return xor_stage(x, "tile", stages[-1])

    doubling = [[1 << n] for n in range(1, tiles.bit_length() - 1)]
    count = frames * spots
    stats = over_tiles(stat, doubling)
    middle, stat_two = call(
        functools.partial(middle_body, len(stats), count),
        (shaped((frames, columns, tile_rows * channels), BF16), shaped((2, 128), F32)),
        flops=flops * 2,
        scratch=[
            pltpu.VMEM((frames, rows, columns, 3 * wide), BF16),
            pltpu.VMEM((frames, spots, 128), F32),
        ],
        n_in=len(stats) + 8,
    )(*stats, *got, first, cached_one, late_one, early_one)

    mids = xor_stage(middle, "src", [1, 2])
    cut = columns // 2
    mids += [xor_send(mids[1][:, :cut], "src", 2), xor_send(mids[2][:, cut:], "src", 1)]
    stats = over_tiles(jnp.stack(xor_stage(stat_two, "src", others)), far_masks(tiles))
    above, below = edges_of(mids[:3] + [jnp.concatenate(mids[3:], axis=1)], channels)
    part, scales = call(
        functools.partial(last_body, len(stats), count),
        (shaped((frames, spots, 128), F32), shaped((2, wide), F32)),
        flops=flops * 2,
        scratch=[pltpu.VMEM((frames, rows, columns, 3 * wide), BF16)],
        n_in=len(stats) + 12,
    )(*stats, *got, *mids, cached_two, late_two, early_two)
    decoded = call(
        edge_body,
        shaped((frames, tile_rows, columns, channels), BF16),
        flops=flops // 2,
        scratch=[
            pltpu.VMEM((frames, 2, columns, 3 * wide), BF16),
            pltpu.VMEM((frames, tile_rows, columns, channels), BF16),
            pltpu.SemaphoreType.DMA((frames,)),
        ],
        n_in=7,
        out_specs=HBM,
    )(part, scales, above, below, first, late_two, early_two)
    return decoded.transpose(0, 1, 3, 2)


def solution(mesh):
    placed = (
        P(None, ("src", "tile"), None, None),
        P(),
        P(None, "tile", None, None),
        P(None, "tile", "src", None),
        P(None, "tile", "src", None),
        P(None, None, None, None, "src"),
        P(None, None, None, "src", None),
        P(None, None, None, "src", None),
        P("src"),
        P("src"),
    )
    return jax.shard_map(
        window,
        mesh=mesh,
        in_specs=placed,
        out_specs=P(None, "tile", "src", None),
        check_vma=False,
    )
```
